128 devices in a mesh: strata: 8 (over y, core), chain: 16 (over z, x).
Axes of the slice: x: 4, y: 4, z: 4, core: 2. Of those that a mesh axis runs over, the one named last changes fastest.
Arguments:
- features: bfloat16 [262144, 512], P(('strata', 'chain')), may hold values from -6 to 6
- events: int32 [262144, 35], P(('strata', 'chain')), may hold values from 0 to 32767, as said below
- tie_first: int32 [262144], P(('strata', 'chain')), may hold values from 0 to 32767, as said below
- entry_row: int32 [262144], P(('strata', 'chain')), may hold values from 0 to 32767, as said below
- w_in: bfloat16 [512, 512], replicated, may hold values from -0.25 to 0.25
- w_mid: bfloat16 [512, 512], replicated, may hold values from -0.25 to 0.25
- w_out: bfloat16 [512, 512], replicated, may hold values from -0.25 to 0.25
Outputs:
- endpoint_loss: float32 [512], replicated
- grad_x: bfloat16 [262144, 512], P(('strata', 'chain'))
- grad_in: float32 [512, 512], replicated
- grad_mid: float32 [512, 512], replicated
- grad_out: float32 [512, 512], replicated
The draws below stay inside these ranges and needn't reach their ends.
Inputs may be any that keep to these rules, and one draw needn't show every extreme that they name: Bit b of events[i, k] is row i's event indicator for endpoint 15 k + b; bits 15 and above, and bits for endpoints 512 and beyond, are zero. Groups of equal stop time are runs of consecutive rows lying inside aligned blocks of 2048 rows; tie_first[i] is the first row of row i's run, counted within its stratum. An interval is at risk at the stop time of row k's group exactly when entry_row <= tie_first[k] and the interval's row is >= tie_first[k]. For every row, tie_first[i] - 2048 < entry_row[i] <= tie_first[i]; in every aligned block of 2048 rows some row has entry_row = max(tie_first - 1 * 2048 + 1, 0).
All inputs are finite; a program needn't handle non-finite values.
Results may differ from the reference program's by a relative error of at most 0.006.
The reference program's roundings to bfloat16 on the way (of `first_hidden`, `hidden`, `eta_grad`, `mid_grad` and `pre_grad`) count: a program that leaves them out, or rounds other values in their place, can miss the bound.
Values sent between devices are 32-bit elements; how exact they have to be, the bound alone decides.
A program may use at most 128 MiB of HBM per device.

```python
from functools import partial
import jax
import jax.numpy as jnp
from jax import lax

FEATURES = 512
HIDDEN_SIZE = 512
ENDPOINTS = 512
BACK = 1
CHAIN_ROWS = 2048
WORDS = 35
STRATA = 8
STRATUM_ROWS = 32768
ROWS = 262144


def tie_groups(key):
    position = jnp.arange(ROWS, dtype=jnp.int32)
    starts = jax.random.randint(jax.random.fold_in(key, 11), (ROWS,), 0, 3) == 0
    starts = jnp.logical_or(starts, position % CHAIN_ROWS == 0)
    marked = jnp.where(starts, position, 0)
    leader = lax.cummax(marked, axis=0)
    return (leader - position // STRATUM_ROWS * STRATUM_ROWS, position)


def draw_tie_first(key, part):
    leader, position = tie_groups(key)
    return leader.astype(jnp.int32)


def draw_entry_row(key, part):
    leader, position = tie_groups(key)
    reach_rows = BACK * CHAIN_ROWS
    first_draw = jax.random.randint(jax.random.fold_in(key, 12), (ROWS,), 0, reach_rows)
    second_draw = jax.random.randint(jax.random.fold_in(key, 17), (ROWS,), 0, reach_rows)
    offset = first_draw * second_draw // reach_rows
    block_count = ROWS // CHAIN_ROWS
    gather_rows = jax.random.randint(jax.random.fold_in(key, 18), (block_count,), CHAIN_ROWS // 2, CHAIN_ROWS)
    block_id = position // CHAIN_ROWS
    earlier_row = jnp.take(gather_rows, jnp.maximum(block_id - 1, 0).astype(jnp.int32))
    inner = leader % CHAIN_ROWS
    usable = jnp.logical_and(leader >= CHAIN_ROWS, earlier_row > inner)
    joined = jax.random.randint(jax.random.fold_in(key, 19), (ROWS,), 0, 4) != 0
    target_row = leader - inner - CHAIN_ROWS + earlier_row
    entry = jnp.where(jnp.logical_and(usable, joined), target_row, jnp.maximum(leader - offset, 0))
    chosen = jax.random.randint(jax.random.fold_in(key, 13), (block_count,), 0, CHAIN_ROWS)
    forced = position % CHAIN_ROWS == jnp.repeat(chosen, CHAIN_ROWS)
    entry = jnp.where(forced, jnp.maximum(leader - reach_rows + 1, 0), entry)
    return entry.astype(jnp.int32)


def draw_events(key, part):
    position = jnp.arange(ROWS, dtype=jnp.int32)[:, None]
    starts = jax.random.randint(jax.random.fold_in(key, 15), (ROWS, ENDPOINTS), 0, 256) == 0
    marked = jnp.where(starts, position, -1000000)
    latest = lax.cummax(marked, axis=0)
    span = jax.random.randint(jax.random.fold_in(key, 16), (1, ENDPOINTS), 96, 224)
    active = position - latest < span
    fired = jax.random.randint(jax.random.fold_in(key, 14), (ROWS, ENDPOINTS), 0, 8) != 0
    event_bits = jnp.logical_and(active, fired).astype(jnp.int32)
    event_bits = jnp.pad(event_bits, ((0, 0), (0, WORDS * 15 - ENDPOINTS)))
    column = jnp.arange(WORDS * 15, dtype=jnp.int32)
    weights = jnp.left_shift(jnp.ones_like(column), column % 15)
    return jnp.sum((event_bits * weights).reshape(ROWS, WORDS, 15), axis=2).astype(jnp.int32)


def level_of(rng, shape, cuts, smallest, high):
    def one(dim, blocks):
        heights = jax.random.uniform(jax.random.fold_in(jax.random.fold_in(rng, 6), dim), (blocks,), jnp.float32, smallest / len(cuts), high / len(cuts))
        return jnp.repeat(jnp.exp(heights), shape[dim] // blocks).reshape((-1,) + (1,) * (len(shape) - dim - 1))

    level = one(*cuts[0])
    for cut in cuts[1:]:
        level = level * one(*cut)
    return level


def normal_values(own_key, dims, deviation, limit, cuts=(), kind=jnp.bfloat16):
    values = deviation * jax.random.normal(own_key, dims, jnp.float32)
    if cuts:
        values = values * level_of(own_key, dims, cuts, -0.22, 0.18)
    return jnp.clip(values, -limit, limit).astype(kind)


def setup_inputs(seed: int = 0) -> dict:
    arg_keys = jax.random.split(jax.random.key(seed), 8)
    features = normal_values(arg_keys[0], (ROWS, FEATURES), 1.0, 6.0, ((0, 128),))
    events = draw_events(jax.random.fold_in(arg_keys[7], 71), 0)
    tie_first = draw_tie_first(jax.random.fold_in(arg_keys[7], 71), 0)
    entry_row = draw_entry_row(jax.random.fold_in(arg_keys[7], 71), 0)
    w_in = normal_values(arg_keys[4], (FEATURES, HIDDEN_SIZE), FEATURES ** -0.5, 0.25)
    w_mid = normal_values(arg_keys[5], (HIDDEN_SIZE, HIDDEN_SIZE), HIDDEN_SIZE ** -0.5, 0.25)
    w_out = normal_values(arg_keys[6], (HIDDEN_SIZE, ENDPOINTS), HIDDEN_SIZE ** -0.5, 0.25)
    return {"features": features, "events": events, "tie_first": tie_first, "entry_row": entry_row, "w_in": w_in, "w_mid": w_mid, "w_out": w_out}


def unpack_events(events, out_width):
    column = jnp.arange(out_width, dtype=jnp.int32)
    spread = jnp.repeat(events, 15, axis=1)[:, :out_width]
    return jnp.bitwise_and(jnp.right_shift(spread, column % 15), 1)


def silu_slope(value):
    sigma = jax.nn.sigmoid(value)
    return sigma * (1.0 + value * (1.0 - sigma))


def stratum_pass(inputs, w_in, w_mid, w_out):
    features, events, tie_first, entry_row = inputs
    preact = jnp.dot(features, w_in, preferred_element_type=jnp.float32)
    first_hidden = jax.nn.silu(preact).astype(jnp.bfloat16)
    mid_pre = jnp.dot(first_hidden, w_mid, preferred_element_type=jnp.float32)
    hidden = jax.nn.silu(mid_pre).astype(jnp.bfloat16)
    log_hazard = jnp.dot(hidden, w_out, preferred_element_type=jnp.float32)
    weight = jnp.exp(log_hazard)
    indicator = unpack_events(events, ENDPOINTS).astype(jnp.float32)
    entered = jax.ops.segment_sum(weight, entry_row, num_segments=STRATUM_ROWS)
    at_risk = lax.cumsum(weight - entered, axis=0, reverse=True) + entered
    divisor = jnp.take(at_risk, tie_first, axis=0)
    loss_terms = jnp.sum(indicator * (jnp.log(divisor) - log_hazard), axis=0)
    hazard = indicator / divisor
    grouped = jax.ops.segment_sum(hazard, tie_first, num_segments=STRATUM_ROWS)
    inclusive = lax.cumsum(grouped, axis=0)
    exclusive = inclusive - grouped
    exposure = inclusive - jnp.take(exclusive, entry_row, axis=0)
    eta_grad = (weight * exposure - indicator).astype(jnp.bfloat16)
    grad_out = jnp.dot(hidden.T, eta_grad, preferred_element_type=jnp.float32)
    hidden_grad = jnp.dot(eta_grad, w_out.T, preferred_element_type=jnp.float32)
    mid_grad = (hidden_grad * silu_slope(mid_pre)).astype(jnp.bfloat16)
    grad_mid = jnp.dot(first_hidden.T, mid_grad, preferred_element_type=jnp.float32)
    first_grad = jnp.dot(mid_grad, w_mid.T, preferred_element_type=jnp.float32)
    pre_grad = (first_grad * silu_slope(preact)).astype(jnp.bfloat16)
    grad_in = jnp.dot(features.T, pre_grad, preferred_element_type=jnp.float32)
    grad_x = jnp.dot(pre_grad, w_in.T, preferred_element_type=jnp.float32).astype(jnp.bfloat16)
    return loss_terms, grad_in, grad_mid, grad_out, grad_x


def reference(features, events, tie_first, entry_row, w_in, w_mid, w_out):
    inputs = (features.reshape(STRATA, STRATUM_ROWS, FEATURES),
              events.reshape(STRATA, STRATUM_ROWS, WORDS),
              tie_first.reshape(STRATA, STRATUM_ROWS),
              entry_row.reshape(STRATA, STRATUM_ROWS))
    loss_terms, grad_in, grad_mid, grad_out, grad_x = lax.map(
        partial(stratum_pass, w_in=w_in, w_mid=w_mid, w_out=w_out), inputs)
    factor = ROWS ** -0.5
    endpoint_loss = jnp.sum(loss_terms, axis=0) / ROWS
    return (endpoint_loss, grad_x.reshape(ROWS, FEATURES),
            jnp.sum(grad_in, axis=0) * factor, jnp.sum(grad_mid, axis=0) * factor,
            jnp.sum(grad_out, axis=0) * factor)
```

```python
import jax
import jax.numpy as jnp
from jax import lax
from jax.experimental import pallas as pl
from jax.experimental.pallas import tpu as pltpu
from jax.sharding import PartitionSpec as P


T = 256
WORD_BITS = 15
F32 = jnp.float32
BF16 = jnp.bfloat16
ONE = lambda mask: jnp.where(mask, 1.0, 0.0).astype(BF16)


def shift(block, distance):
    devices = range(lax.axis_size("chain"))
    route = [(i, i + distance) for i in devices if i + distance in devices]
    return lax.ppermute(block, "chain", route)


def sigmoid(v):
    return 0.5 * jnp.tanh(0.5 * v) + 0.5


def indicators(ev, spread, bit):
    hi = lax.shift_right_logical(ev, 8).astype(F32).astype(BF16)
    lo = jnp.bitwise_and(ev, 255).astype(F32).astype(BF16)
    word = jnp.dot(hi, spread, preferred_element_type=F32) * 256.0
    word = word + jnp.dot(lo, spread, preferred_element_type=F32)
    return jnp.bitwise_and(lax.shift_right_logical(word.astype(jnp.int32), bit), 1).astype(F32)


def forward_kernel(x, ev, w_in, w_mid, w_out, spread, bit, fh, s1, hid, s2, ind, wb, part, *w_parts):
    pre = jnp.dot(x[...], w_in[...], preferred_element_type=F32)
    s = sigmoid(pre)
    first = (pre * s).astype(BF16)
    fh[...] = first
    s1[...] = (s * (1.0 + pre * (1.0 - s))).astype(BF16)
    mid = jnp.dot(first, w_mid[...], preferred_element_type=F32)
    s = sigmoid(mid)
    hidden = (mid * s).astype(BF16)
    hid[...] = hidden
    s2[...] = (s * (1.0 + mid * (1.0 - s))).astype(BF16)
    eta = jnp.dot(hidden, w_out[...], preferred_element_type=F32)
    weight = jnp.exp(eta)
    wb[...] = weight.astype(BF16)
    width = w_parts[0].shape[1]
    for c, ref in enumerate(w_parts):
        ref[...] = weight[:, c * width : (c + 1) * width]
    flag = indicators(ev[...], spread[...], bit[...])
    ind[...] = flag.astype(BF16)

    @pl.when(pl.program_id(0) == 0)
    def _():
        part[...] = jnp.zeros_like(part)

    part[...] += jnp.sum((flag * eta).reshape(-1, 8, eta.shape[1]), axis=0)


def unpack_kernel(ev, spread, bit, ind):
    ind[...] = indicators(ev[...], spread[...], bit[...]).astype(BF16)


ENTRY, ENTRY_N, ENTRY_P, FIRST, FIRST_P = range(5)
FMIN, FMAX, FPMIN, FPMAX, EMIN, ENMIN, EPMIN = range(7)


def tile(i):
    return pl.ds(pl.multiple_of(i * T, T), T)


def lanes(build):
    return jnp.concatenate([build(h) for h in range(T // 128)], axis=1)


def row_of(rows, k, tile_id, h):
    return rows[k : k + 1, tile_id * T + h * 128 : tile_id * T + (h + 1) * 128]


def own_kernel(bounds, rows, first_col, firstp_col, wb, own, prev, acc):
    n = rows.shape[1] // T

    def b(kind, t):
        return bounds[kind * n + t]

    def step(i, _):
        at = tile(i)
        first = first_col[at, :]
        acc[...] = jnp.zeros_like(acc)
        for j in range(n):
            @pl.when((b(EMIN, j) <= b(FMAX, i)) & (b(FMIN, i) <= j * T + T - 1))
            def _():
                def build(h):
                    col = lax.broadcasted_iota(jnp.int32, (T, 128), 1) + (j * T + h * 128)
                    return ONE((row_of(rows, ENTRY, j, h) <= first) & (first <= col))

                acc[...] += jnp.dot(lanes(build), wb[j * T : (j + 1) * T, :], preferred_element_type=F32)

        own[at, :] = acc[...]
        firstp = firstp_col[at, :]
        acc[...] = jnp.zeros_like(acc)
        for j in range(n):
            @pl.when(b(EMIN, j) <= b(FPMAX, i))
            def _():
                mask = lanes(lambda h: ONE(row_of(rows, ENTRY, j, h) <= firstp))
                acc[...] += jnp.dot(mask, wb[j * T : (j + 1) * T, :], preferred_element_type=F32)

        prev[at, :] = acc[...]
        return 0

    lax.fori_loop(0, n, step, 0)


def risk_kernel(
    bounds, rows, first_col, firstp_col, entry_col, own, prev, ind, indp, w, wn, wp,
    eta, part, acc, wnb, wpb, hb, hp,
):
    n = rows.shape[1] // T

    def b(kind, t):
        return bounds[kind * n + t]

    wnb[...] = wn[...].astype(BF16)
    wpb[...] = wp[...].astype(BF16)
    part[...] = jnp.zeros_like(part)

    def hazards(i, _):
        at = tile(i)
        first = first_col[at, :]
        acc[...] = own[at, :]
        for j in range(n):
            @pl.when(b(ENMIN, j) <= b(FMAX, i))
            def _():
                mask = lanes(lambda h: ONE(row_of(rows, ENTRY_N, j, h) <= first))
                acc[...] += jnp.dot(mask, wnb[j * T : (j + 1) * T, :], preferred_element_type=F32)

        divisor = acc[...]
        flag = ind[at, :].astype(F32) > 0.0
        hb[at, :] = jnp.where(flag, 1.0 / divisor, 0.0).astype(BF16)
        logs = jnp.where(flag, jnp.log(divisor), 0.0)
        part[...] += jnp.sum(logs.reshape(-1, 8, logs.shape[1]), axis=0)
        firstp = firstp_col[at, :]
        acc[...] = prev[at, :]
        for j in range(n):
            @pl.when((b(EPMIN, j) <= b(FPMAX, i)) & (b(FPMIN, i) <= j * T + T - 1 - n * T))
            def _():
                def build(h):
                    col = lax.broadcasted_iota(jnp.int32, (T, 128), 1) + (j * T + h * 128 - n * T)
                    return ONE((row_of(rows, ENTRY_P, j, h) <= firstp) & (firstp <= col))

                acc[...] += jnp.dot(lanes(build), wpb[j * T : (j + 1) * T, :], preferred_element_type=F32)

        flagp = indp[at, :].astype(F32) > 0.0
        hp[at, :] = jnp.where(flagp, 1.0 / acc[...], 0.0).astype(BF16)
        return 0

    lax.fori_loop(0, n, hazards, 0)

    def gradient(j, _):
        at = tile(j)
        entry = entry_col[at, :]
        here = lax.broadcasted_iota(jnp.int32, (T, 128), 0) + j * T
        acc[...] = jnp.zeros_like(acc)
        for i in range(n):
            @pl.when((b(EMIN, j) <= b(FMAX, i)) & (b(FMIN, i) <= j * T + T - 1))
            def _():
                def build(h):
                    first = row_of(rows, FIRST, i, h)
                    return ONE((entry <= first) & (first <= here))

                acc[...] += jnp.dot(lanes(build), hb[i * T : (i + 1) * T, :], preferred_element_type=F32)

            @pl.when(b(EMIN, j) <= b(FPMAX, i))
            def _():
                mask = lanes(lambda h: ONE(entry <= row_of(rows, FIRST_P, i, h)))
                acc[...] += jnp.dot(mask, hp[i * T : (i + 1) * T, :], preferred_element_type=F32)

        eta[at, :] = (w[at, :] * acc[...] - ind[at, :].astype(F32)).astype(BF16)
        return 0

    lax.fori_loop(0, n, gradient, 0)


def on_device(features, events, tie_first, entry_row, w_in, w_mid, w_out):
    rows, width = features.shape[0], w_in.shape[0]
    hidden_width, out_width = w_out.shape
    words = events.shape[1]
    chain, strata = lax.axis_size("chain"), lax.axis_size("strata")
    total_rows = rows * chain * strata
    tiles = rows // T
    parts = 2
    part_width = out_width // parts
    start = lax.axis_index("chain") * rows

    index = jnp.stack([tie_first, entry_row])
    indexp = shift(index, 1)
    index_n = shift(entry_row, -1)
    eventsp = shift(events, 1)
    first, entry = tie_first - start, entry_row - start
    firstp, entryp = indexp[0] - start, indexp[1] - start
    entryn = index_n - start
    table = jnp.stack([entry, entryn, entryp, first, firstp, firstp, firstp, firstp])

    def low(v):
        return jnp.min(v.reshape(tiles, T), axis=1)

    def high(v):
        return jnp.max(v.reshape(tiles, T), axis=1)

    bounds = jnp.concatenate(
        [low(first), high(first), low(firstp), high(firstp), low(entry), low(entryn), low(entryp)]
    )
    first_col = jnp.broadcast_to(first[:, None], (rows, 128))
    firstp_col = jnp.broadcast_to(firstp[:, None], (rows, 128))
    entry_col = jnp.broadcast_to(entry[:, None], (rows, 128))
    column = jnp.arange(out_width, dtype=jnp.int32)
    spread = (column[None, :] // WORD_BITS == jnp.arange(words, dtype=jnp.int32)[:, None]).astype(BF16)
    bit = (column % WORD_BITS)[None, :]

    def whole(shape):
        return pl.BlockSpec(shape, lambda i: (0, 0))

    def by_rows(cols):
        return pl.BlockSpec((T, cols), lambda i: (i, 0))

    def array(cols, kind):
        return jax.ShapeDtypeStruct((rows, cols), kind)

    fh, s1, hidden, s2, ind, wb, part_eta, *weights = pl.pallas_call(
        forward_kernel,
        grid=(tiles,),
        in_specs=[by_rows(width), by_rows(words), whole(w_in.shape), whole(w_mid.shape), whole(w_out.shape),
                  whole(spread.shape), whole(bit.shape)],
        out_specs=[by_rows(hidden_width)] * 4 + [by_rows(out_width)] * 2 + [whole((8, out_width))]
        + [by_rows(part_width)] * parts,
        out_shape=[array(hidden_width, BF16)] * 4 + [array(out_width, BF16)] * 2
        + [jax.ShapeDtypeStruct((8, out_width), F32)] + [array(part_width, F32)] * parts,
        name="forward",
    )(features, events, w_in, w_mid, w_out, spread, bit)

    nexts = [shift(w, -1) for w in weights]
    prevs = [shift(w, 1) for w in weights]

    indp = pl.pallas_call(
        unpack_kernel,
        grid=(tiles,),
        in_specs=[by_rows(words), whole(spread.shape), whole(bit.shape)],
        out_specs=by_rows(out_width),
        out_shape=array(out_width, BF16),
        name="unpack",
    )(eventsp, spread, bit)

    vmem = pl.BlockSpec(memory_space=pltpu.VMEM)
    smem = pl.BlockSpec(memory_space=pltpu.SMEM)
    own, prev = pl.pallas_call(
        own_kernel,
        in_specs=[smem] + [vmem] * 4,
        out_specs=[vmem] * 2,
        out_shape=[array(out_width, F32)] * 2,
        scratch_shapes=[pltpu.VMEM((T, out_width), F32)],
        name="own",
    )(bounds, table, first_col, firstp_col, wb)

    etas, logs = [], []
    for c in range(parts):
        cols = slice(c * part_width, (c + 1) * part_width)
        eta, log_part = pl.pallas_call(
            risk_kernel,
            in_specs=[smem] + [vmem] * 11,
            out_specs=[vmem] * 2,
            out_shape=[array(part_width, BF16), jax.ShapeDtypeStruct((8, part_width), F32)],
            scratch_shapes=[pltpu.VMEM((T, part_width), F32)] + [pltpu.VMEM((rows, part_width), BF16)] * 4,
            name="risk",
        )(bounds, table, first_col, firstp_col, entry_col, own[:, cols], prev[:, cols], ind[:, cols],
          indp[:, cols], weights[c], nexts[c], prevs[c])
        etas.append(eta)
        logs.append(log_part)

    factor = total_rows ** (-0.5)
    loss_part = (jnp.sum(jnp.concatenate(logs, axis=1), axis=0) - jnp.sum(part_eta, axis=0)) / total_rows
    eta_grad = jnp.concatenate(etas, axis=1)
    grad_out = jnp.einsum("rh,re->he", hidden, eta_grad, preferred_element_type=F32) * factor
    hidden_grad = jnp.einsum("re,he->rh", eta_grad, w_out, preferred_element_type=F32)
    mid_grad = (hidden_grad * s2.astype(F32)).astype(BF16)
    grad_mid = jnp.einsum("rg,rh->gh", fh, mid_grad, preferred_element_type=F32) * factor
    first_grad = jnp.einsum("rh,gh->rg", mid_grad, w_mid, preferred_element_type=F32)
    pre_grad = (first_grad * s1.astype(F32)).astype(BF16)
    grad_in = jnp.einsum("rf,rh->fh", features, pre_grad, preferred_element_type=F32) * factor
    grad_x = jnp.einsum("rh,fh->rf", pre_grad, w_in, preferred_element_type=F32).astype(BF16)
    grad_in, grad_mid, grad_out, endpoint_loss = lax.psum(
        (grad_in, grad_mid, grad_out, loss_part), ("strata", "chain")
    )
    return (endpoint_loss, grad_x, grad_in, grad_mid, grad_out)


def solution(mesh):
    placed = (
        P(("strata", "chain"), None),
        P(("strata", "chain"), None),
        P(("strata", "chain")),
        P(("strata", "chain")),
        P(),
        P(),
        P(),
    )
    return jax.shard_map(
        on_device,
        mesh=mesh,
        in_specs=placed,
        out_specs=(P(), P(("strata", "chain"), None), P(), P(), P()),
        check_vma=False,
    )
```

```python
import jax
import jax.numpy as jnp
from jax import lax
from jax.experimental import pallas as pl
from jax.experimental.pallas import tpu as pltpu
from jax.sharding import PartitionSpec as P


T = 256
WORD_BITS = 15
F32 = jnp.float32
BF16 = jnp.bfloat16
MESH = pl.DeviceIdType.MESH
ONE = lambda mask: jnp.where(mask, 1.0, 0.0).astype(BF16)


def shift(block, distance):
    devices = range(lax.axis_size("chain"))
    route = [(i, i + distance) for i in devices if i + distance in devices]
    return lax.ppermute(block, "chain", route)


def sigmoid(v):
    return 0.5 * jnp.tanh(0.5 * v) + 0.5


def indicators(ev, spread, bit):
    hi = lax.shift_right_logical(ev, 8).astype(F32).astype(BF16)
    lo = jnp.bitwise_and(ev, 255).astype(F32).astype(BF16)
    word = jnp.dot(hi, spread, preferred_element_type=F32) * 256.0
    word = word + jnp.dot(lo, spread, preferred_element_type=F32)
    return jnp.bitwise_and(lax.shift_right_logical(word.astype(jnp.int32), bit), 1).astype(F32)


def forward_kernel(x, ev, w_in, w_mid, w_out, spread, bit, fh, s1, hid, s2, ind, wb, part, *w_parts):
    pre = jnp.dot(x[...], w_in[...], preferred_element_type=F32)
    s = sigmoid(pre)
    first = (pre * s).astype(BF16)
    fh[...] = first
    s1[...] = (s * (1.0 + pre * (1.0 - s))).astype(BF16)
    mid = jnp.dot(first, w_mid[...], preferred_element_type=F32)
    s = sigmoid(mid)
    hidden = (mid * s).astype(BF16)
    hid[...] = hidden
    s2[...] = (s * (1.0 + mid * (1.0 - s))).astype(BF16)
    eta = jnp.dot(hidden, w_out[...], preferred_element_type=F32)
    weight = jnp.exp(eta)
    wb[...] = weight.astype(BF16)
    width = w_parts[0].shape[1]
    for c, ref in enumerate(w_parts):
        ref[...] = weight[:, c * width : (c + 1) * width]
    flag = indicators(ev[...], spread[...], bit[...])
    ind[...] = flag.astype(BF16)

    @pl.when(pl.program_id(0) == 0)
    def _():
        part[...] = jnp.zeros_like(part)

    part[...] += jnp.sum((flag * eta).reshape(-1, 8, eta.shape[1]), axis=0)


def unpack_kernel(ev, spread, bit, ind):
    ind[...] = indicators(ev[...], spread[...], bit[...]).astype(BF16)


ENTRY, ENTRY_N, ENTRY_P, FIRST, FIRST_P = range(5)
FMIN, FMAX, FPMIN, FPMAX, EMIN, ENMIN, EPMIN = range(7)


def tile(i):
    return pl.ds(pl.multiple_of(i * T, T), T)


def lanes(build):
    return jnp.concatenate([build(h) for h in range(T // 128)], axis=1)


def row_of(rows, k, tile_id, h):
    return rows[k : k + 1, tile_id * T + h * 128 : tile_id * T + (h + 1) * 128]


def own_kernel(bounds, rows, first_col, firstp_col, wb, own, prev, acc):
    n = rows.shape[1] // T

    def b(kind, t):
        return bounds[kind * n + t]

    def step(i, _):
        at = tile(i)
        first = first_col[at, :]
        acc[...] = jnp.zeros_like(acc)
        for j in range(n):
            @pl.when((b(EMIN, j) <= b(FMAX, i)) & (b(FMIN, i) <= j * T + T - 1))
            def _():
                def build(h):
                    col = lax.broadcasted_iota(jnp.int32, (T, 128), 1) + (j * T + h * 128)
                    return ONE((row_of(rows, ENTRY, j, h) <= first) & (first <= col))

                acc[...] += jnp.dot(lanes(build), wb[j * T : (j + 1) * T, :], preferred_element_type=F32)

        own[at, :] = acc[...]
        firstp = firstp_col[at, :]
        acc[...] = jnp.zeros_like(acc)
        for j in range(n):
            @pl.when(b(EMIN, j) <= b(FPMAX, i))
            def _():
                mask = lanes(lambda h: ONE(row_of(rows, ENTRY, j, h) <= firstp))
                acc[...] += jnp.dot(mask, wb[j * T : (j + 1) * T, :], preferred_element_type=F32)

        prev[at, :] = acc[...]
        return 0

    lax.fori_loop(0, n, step, 0)


def risk_kernel(
    bounds, rows, first_col, firstp_col, entry_col, own, prev, ind, indp, w, wn, wp,
    eta, part, acc, wnb, wpb, hb, hp,
):
    n = rows.shape[1] // T

    def b(kind, t):
        return bounds[kind * n + t]

    wnb[...] = wn[...].astype(BF16)
    wpb[...] = wp[...].astype(BF16)
    part[...] = jnp.zeros_like(part)

    def hazards(i, _):
        at = tile(i)
        first = first_col[at, :]
        acc[...] = own[at, :]
        for j in range(n):
            @pl.when(b(ENMIN, j) <= b(FMAX, i))
            def _():
                mask = lanes(lambda h: ONE(row_of(rows, ENTRY_N, j, h) <= first))
                acc[...] += jnp.dot(mask, wnb[j * T : (j + 1) * T, :], preferred_element_type=F32)

        divisor = acc[...]
        flag = ind[at, :].astype(F32) > 0.0
        hb[at, :] = jnp.where(flag, 1.0 / divisor, 0.0).astype(BF16)
        logs = jnp.where(flag, jnp.log(divisor), 0.0)
        part[...] += jnp.sum(logs.reshape(-1, 8, logs.shape[1]), axis=0)
        firstp = firstp_col[at, :]
        acc[...] = prev[at, :]
        for j in range(n):
            @pl.when((b(EPMIN, j) <= b(FPMAX, i)) & (b(FPMIN, i) <= j * T + T - 1 - n * T))
            def _():
                def build(h):
                    col = lax.broadcasted_iota(jnp.int32, (T, 128), 1) + (j * T + h * 128 - n * T)
                    return ONE((row_of(rows, ENTRY_P, j, h) <= firstp) & (firstp <= col))

                acc[...] += jnp.dot(lanes(build), wpb[j * T : (j + 1) * T, :], preferred_element_type=F32)

        flagp = indp[at, :].astype(F32) > 0.0
        hp[at, :] = jnp.where(flagp, 1.0 / acc[...], 0.0).astype(BF16)
        return 0

    lax.fori_loop(0, n, hazards, 0)

    def gradient(j, _):
        at = tile(j)
        entry = entry_col[at, :]
        here = lax.broadcasted_iota(jnp.int32, (T, 128), 0) + j * T
        acc[...] = jnp.zeros_like(acc)
        for i in range(n):
            @pl.when((b(EMIN, j) <= b(FMAX, i)) & (b(FMIN, i) <= j * T + T - 1))
            def _():
                def build(h):
                    first = row_of(rows, FIRST, i, h)
                    return ONE((entry <= first) & (first <= here))

                acc[...] += jnp.dot(lanes(build), hb[i * T : (i + 1) * T, :], preferred_element_type=F32)

            @pl.when(b(EMIN, j) <= b(FPMAX, i))
            def _():
                mask = lanes(lambda h: ONE(entry <= row_of(rows, FIRST_P, i, h)))
                acc[...] += jnp.dot(mask, hp[i * T : (i + 1) * T, :], preferred_element_type=F32)

        eta[at, :] = (w[at, :] * acc[...] - ind[at, :].astype(F32)).astype(BF16)
        return 0

    lax.fori_loop(0, n, gradient, 0)


def coordinates():
    s, c = lax.axis_index("strata"), lax.axis_index("chain")
    return {"y": s // 2, "core": s % 2, "z": c // 4, "x": c % 4}


def device(at, **moved):
    at = {**at, **moved}
    return (at["y"] * 2 + at["core"], at["z"] * 4 + at["x"])


def reduce_kernel(*refs):
    m = 3
    given, loss, outs, loss_out = refs[:m], refs[m], refs[m + 1 : 2 * m + 1], refs[2 * m + 1]
    acc, pair, half, quarter, two, three, tally, send, recv = refs[2 * m + 2 :]
    at = coordinates()
    core = at["core"]
    half_rows = acc.shape[1]

    barrier = pltpu.get_barrier_semaphore()
    friends = [device(at, core=1 - core)]
    for axis in "xyz":
        friends += [device(at, **{axis: (at[axis] + d) % 4}) for d in range(1, 4)]
    for friend in friends:
        pl.semaphore_signal(barrier, inc=1, device_id=friend, device_id_type=MESH)
    pl.semaphore_wait(barrier, len(friends))

    count = iter(range(send.shape[0]))
    flying = []

    def put(source, target, to):
        k = next(count)
        copy = pltpu.make_async_remote_copy(
            src_ref=source, dst_ref=target, send_sem=send.at[k], recv_sem=recv.at[k],
            device_id=to, device_id_type=MESH,
        )
        copy.start()
        flying.append(copy)
        return copy

    def rows(offset, size):
        return pl.ds(pl.multiple_of(offset, 8), size)

    class Stream:
        pass

    streams = []
    for t in range(m):
        s = Stream()
        s.t = t
        s.axes = ["xyz"[(t + k) % 3] for k in range(3)]
        p = at[s.axes[0]]
        high = p // 2
        low = (p + high) % 2
        s.near, s.far = (p // 2) * 2 + (1 - p % 2), 3 - p
        s.bits = [(low, high), (high, low)]
        s.partners = [(s.near, s.far), (s.far, s.near)]
        s.offset = [low * 64 + high * 32, 128 + high * 64 + low * 32]
        streams.append(s)

    axes_of_tally = ["core", "x", "y", "z"]

    def tally_send(k):
        axis = axes_of_tally[k]
        n = 2 if axis == "core" else 4
        return [
            put(tally.at[k, at[axis]], tally.at[k, at[axis]], device(at, **{axis: (at[axis] + d) % n}))
            for d in range(1, n)
        ]

    def tally_sum(k, copies):
        for copy in copies:
            copy.wait_recv()
        total = tally[k, 0]
        for slot in range(1, 2 if k == 0 else 4):
            total = total + tally[k, slot]
        return total

    tally[0, core] = loss[...]
    tally_copies = tally_send(0)
    for s in streams:
        s.copies = [put(given[s.t].at[rows((1 - core) * half_rows, half_rows)], pair.at[s.t], device(at, core=1 - core))]
    for s in streams:
        s.copies[0].wait_recv()
        acc[s.t] = given[s.t][rows(core * half_rows, half_rows), :] + pair[s.t]
        s.copies = []
        for u in range(2):
            away = 128 * u + (1 - s.bits[u][0]) * 64
            s.copies.append(put(acc.at[s.t, rows(away, 64)], half.at[s.t, u], device(at, **{s.axes[0]: s.partners[u][0]})))
    total = tally_sum(0, tally_copies)
    tally[1, at["x"]] = total
    tally_copies = tally_send(1)
    for s in streams:
        copies = []
        for u in range(2):
            s.copies[u].wait_recv()
            kept = rows(128 * u + s.bits[u][0] * 64, 64)
            acc[s.t, kept] = acc[s.t, kept] + half[s.t, u]
            away = 128 * u + s.bits[u][0] * 64 + (1 - s.bits[u][1]) * 32
            copies.append(put(acc.at[s.t, rows(away, 32)], quarter.at[s.t, u], device(at, **{s.axes[0]: s.partners[u][1]})))
        s.copies = copies
    total = tally_sum(1, tally_copies)
    tally[2, at["y"]] = total
    tally_copies = tally_send(2)
    for s in streams:
        q = at[s.axes[1]]
        copies = []
        for u in range(2):
            s.copies[u].wait_recv()
            kept = rows(s.offset[u], 32)
            acc[s.t, kept] = acc[s.t, kept] + quarter[s.t, u]
            for d in range(1, 4):
                to = (q + d) % 4
                copies.append(put(acc.at[s.t, rows(s.offset[u] + to * 8, 8)], two.at[s.t, q, pl.ds(u * 8, 8)],
                                  device(at, **{s.axes[1]: to})))
            two[s.t, q, u * 8 : u * 8 + 8] = acc[s.t, rows(s.offset[u] + q * 8, 8)]
        s.copies = copies
    total = tally_sum(2, tally_copies)
    tally[3, at["z"]] = total
    tally_copies = tally_send(3)
    for s in streams:
        r = at[s.axes[2]]
        for copy in s.copies:
            copy.wait_recv()
        three[s.t, r] = two[s.t, 0] + two[s.t, 1] + two[s.t, 2] + two[s.t, 3]
        s.copies = [put(three.at[s.t, r], three.at[s.t, r], device(at, **{s.axes[2]: (r + d) % 4})) for d in range(1, 4)]
    loss_out[...] = tally_sum(3, tally_copies)
    base = core * half_rows
    for s in streams:
        q = at[s.axes[1]]
        for copy in s.copies:
            copy.wait_recv()
        final = three[s.t, 0] + three[s.t, 1] + three[s.t, 2] + three[s.t, 3]
        s.copies = []
        for u in range(2):
            piece = rows(base + s.offset[u] + q * 8, 8)
            outs[s.t][piece, :] = final[u * 8 : u * 8 + 8]
            for d in range(1, 4):
                s.copies.append(put(outs[s.t].at[piece], outs[s.t].at[piece], device(at, **{s.axes[1]: (q + d) % 4})))
    for s in streams:
        for copy in s.copies:
            copy.wait_recv()
        s.copies = []
        for u in range(2):
            piece = rows(base + s.offset[u], 32)
            s.copies.append(put(outs[s.t].at[piece], outs[s.t].at[piece], device(at, **{s.axes[0]: s.partners[u][1]})))
    for s in streams:
        copies = []
        for u in range(2):
            s.copies[u].wait_recv()
            piece = rows(base + 128 * u + s.bits[u][0] * 64, 64)
            copies.append(put(outs[s.t].at[piece], outs[s.t].at[piece], device(at, **{s.axes[0]: s.partners[u][0]})))
        s.copies = copies
    for s in streams:
        for copy in s.copies:
            copy.wait_recv()
        piece = rows(base, half_rows)
        s.copies = [put(outs[s.t].at[piece], outs[s.t].at[piece], device(at, core=1 - core))]
    for s in streams:
        s.copies[0].wait_recv()
    for copy in flying:
        copy.wait_send()


def all_reduce(matrices, loss):
    size = matrices[0].shape
    assert size == (512, 512)
    vmem = pl.BlockSpec(memory_space=pltpu.VMEM)
    m, width = len(matrices), size[1]
    shapes = [(m, 256, width), (m, 256, width), (m, 2, 64, width), (m, 2, 32, width), (m, 4, 16, width),
              (m, 4, 16, width), (4, 4, 8, width)]
    messages = m * (1 + 2 + 2 + 6 + 3 + 6 + 2 + 2 + 1) + 10
    return pl.pallas_call(
        reduce_kernel,
        in_specs=[vmem] * (m + 1),
        out_specs=[vmem] * (m + 1),
        out_shape=[jax.ShapeDtypeStruct(size, F32)] * m + [jax.ShapeDtypeStruct(loss.shape, F32)],
        scratch_shapes=[pltpu.VMEM(shape, F32) for shape in shapes] + [pltpu.SemaphoreType.DMA((messages,))] * 2,
        compiler_params=pltpu.CompilerParams(collective_id=0, has_side_effects=True),
        name="all_reduce",
    )(*matrices, loss)


def on_device(features, events, tie_first, entry_row, w_in, w_mid, w_out):
    rows, width = features.shape[0], w_in.shape[0]
    hidden_width, out_width = w_out.shape
    words = events.shape[1]
    chain, strata = lax.axis_size("chain"), lax.axis_size("strata")
    total_rows = rows * chain * strata
    tiles = rows // T
    parts = 2
    part_width = out_width // parts
    start = lax.axis_index("chain") * rows

    index = jnp.stack([tie_first, entry_row])
    indexp = shift(index, 1)
    index_n = shift(entry_row, -1)
    eventsp = shift(events, 1)
    first, entry = tie_first - start, entry_row - start
    firstp, entryp = indexp[0] - start, indexp[1] - start
    entryn = index_n - start
    table = jnp.stack([entry, entryn, entryp, first, firstp, firstp, firstp, firstp])

    def low(v):
        return jnp.min(v.reshape(tiles, T), axis=1)

    def high(v):
        return jnp.max(v.reshape(tiles, T), axis=1)

    bounds = jnp.concatenate(
        [low(first), high(first), low(firstp), high(firstp), low(entry), low(entryn), low(entryp)]
    )
    first_col = jnp.broadcast_to(first[:, None], (rows, 128))
    firstp_col = jnp.broadcast_to(firstp[:, None], (rows, 128))
    entry_col = jnp.broadcast_to(entry[:, None], (rows, 128))
    column = jnp.arange(out_width, dtype=jnp.int32)
    spread = (column[None, :] // WORD_BITS == jnp.arange(words, dtype=jnp.int32)[:, None]).astype(BF16)
    bit = (column % WORD_BITS)[None, :]

    def whole(shape):
        return pl.BlockSpec(shape, lambda i: (0, 0))

    def by_rows(cols):
        return pl.BlockSpec((T, cols), lambda i: (i, 0))

    def array(cols, kind):
        return jax.ShapeDtypeStruct((rows, cols), kind)

    fh, s1, hidden, s2, ind, wb, part_eta, *weights = pl.pallas_call(
        forward_kernel,
        grid=(tiles,),
        in_specs=[by_rows(width), by_rows(words), whole(w_in.shape), whole(w_mid.shape), whole(w_out.shape),
                  whole(spread.shape), whole(bit.shape)],
        out_specs=[by_rows(hidden_width)] * 4 + [by_rows(out_width)] * 2 + [whole((8, out_width))]
        + [by_rows(part_width)] * parts,
        out_shape=[array(hidden_width, BF16)] * 4 + [array(out_width, BF16)] * 2
        + [jax.ShapeDtypeStruct((8, out_width), F32)] + [array(part_width, F32)] * parts,
        name="forward",
    )(features, events, w_in, w_mid, w_out, spread, bit)

    nexts = [shift(w, -1) for w in weights]
    prevs = [shift(w, 1) for w in weights]

    indp = pl.pallas_call(
        unpack_kernel,
        grid=(tiles,),
        in_specs=[by_rows(words), whole(spread.shape), whole(bit.shape)],
        out_specs=by_rows(out_width),
        out_shape=array(out_width, BF16),
        name="unpack",
    )(eventsp, spread, bit)

    vmem = pl.BlockSpec(memory_space=pltpu.VMEM)
    smem = pl.BlockSpec(memory_space=pltpu.SMEM)
    own, prev = pl.pallas_call(
        own_kernel,
        in_specs=[smem] + [vmem] * 4,
        out_specs=[vmem] * 2,
        out_shape=[array(out_width, F32)] * 2,
        scratch_shapes=[pltpu.VMEM((T, out_width), F32)],
        name="own",
    )(bounds, table, first_col, firstp_col, wb)

    etas, logs = [], []
    for c in range(parts):
        cols = slice(c * part_width, (c + 1) * part_width)
        eta, log_part = pl.pallas_call(
            risk_kernel,
            in_specs=[smem] + [vmem] * 11,
            out_specs=[vmem] * 2,
            out_shape=[array(part_width, BF16), jax.ShapeDtypeStruct((8, part_width), F32)],
            scratch_shapes=[pltpu.VMEM((T, part_width), F32)] + [pltpu.VMEM((rows, part_width), BF16)] * 4,
            name="risk",
        )(bounds, table, first_col, firstp_col, entry_col, own[:, cols], prev[:, cols], ind[:, cols],
          indp[:, cols], weights[c], nexts[c], prevs[c])
        etas.append(eta)
        logs.append(log_part)

    factor = total_rows ** (-0.5)
    loss_part = (jnp.concatenate(logs, axis=1) - part_eta) / total_rows
    eta_grad = jnp.concatenate(etas, axis=1)
    grad_out = jnp.einsum("rh,re->he", hidden, eta_grad, preferred_element_type=F32) * factor
    hidden_grad = jnp.einsum("re,he->rh", eta_grad, w_out, preferred_element_type=F32)
    mid_grad = (hidden_grad * s2.astype(F32)).astype(BF16)
    grad_mid = jnp.einsum("rg,rh->gh", fh, mid_grad, preferred_element_type=F32) * factor
    first_grad = jnp.einsum("rh,gh->rg", mid_grad, w_mid, preferred_element_type=F32)
    pre_grad = (first_grad * s1.astype(F32)).astype(BF16)
    grad_in = jnp.einsum("rf,rh->fh", features, pre_grad, preferred_element_type=F32) * factor
    grad_x = jnp.einsum("rh,fh->rf", pre_grad, w_in, preferred_element_type=F32).astype(BF16)
    grad_in, grad_mid, grad_out, loss_sum = all_reduce((grad_in, grad_mid, grad_out), loss_part)
    endpoint_loss = jnp.sum(loss_sum, axis=0)
    return (endpoint_loss, grad_x, grad_in, grad_mid, grad_out)


def solution(mesh):
    placed = (
        P(("strata", "chain"), None),
        P(("strata", "chain"), None),
        P(("strata", "chain")),
        P(("strata", "chain")),
        P(),
        P(),
        P(),
    )
    return jax.shard_map(
        on_device,
        mesh=mesh,
        in_specs=placed,
        out_specs=(P(), P(("strata", "chain"), None), P(), P(), P()),
        check_vma=False,
    )
```

```python
import functools

import jax
import jax.numpy as jnp
import numpy as np
from jax import lax
from jax.experimental import pallas as pl
from jax.experimental.pallas import tpu as pltpu
from jax.sharding import PartitionSpec as P

T = 256
Q = 512
WORD_BITS = 15
F32 = jnp.float32
BF16 = jnp.bfloat16
I32 = jnp.int32
MESH = pl.DeviceIdType.MESH


def sigmoid(v):
    return 0.5 * jnp.tanh(0.5 * v) + 0.5


def span(i, size):
    return pl.ds(pl.multiple_of(i * size, size), size)


def dot(a, b, contract=((1,), (0,))):
    return lax.dot_general(a, b, (contract, ((), ())), preferred_element_type=F32)


def mask(build):
    return jnp.concatenate([jnp.where(build(h), 1.0, 0.0).astype(BF16) for h in range(Q // 128)], axis=1)


def unpack(words, table):
    hi = lax.shift_right_logical(words, 8).astype(F32).astype(BF16)
    lo = jnp.bitwise_and(words, 255).astype(F32).astype(BF16)
    value = dot(hi, table, ((0,), (0,))) * 256.0 + dot(lo, table, ((0,), (0,)))
    return value.astype(I32)


def coordinates():
    s, c = lax.axis_index("strata"), lax.axis_index("chain")
    return {"y": s // 2, "core": s % 2, "z": c // 4, "x": c % 4}


def device(at, **moved):
    at = {**at, **moved}
    return (at["y"] * 2 + at["core"], at["z"] * 4 + at["x"])


def reduce_all(given, factor, outs, loss_out, acc, pair, half, quarter, two, three, tally, send, recv, at, meanwhile):
    m = len(given)
    core = at["core"]
    half_rows = acc.shape[1]
    count = iter(range(send.shape[0]))
    flying = []

    def put(source, target, to):
        k = next(count)
        copy = pltpu.make_async_remote_copy(
            src_ref=source, dst_ref=target, send_sem=send.at[k], recv_sem=recv.at[k],
            device_id=to, device_id_type=MESH,
        )
        copy.start()
        flying.append(copy)
        return copy

    def rows(offset, size):
        return pl.ds(pl.multiple_of(offset, 8), size)

    class Stream:
        pass

    streams = []
    for t in range(m):
        s = Stream()
        s.t = t
        s.axes = ["xyz"[(t + k) % 3] for k in range(3)]
        p = at[s.axes[0]]
        high = p // 2
        low = (p + high) % 2
        s.near, s.far = (p // 2) * 2 + (1 - p % 2), 3 - p
        s.bits = [(low, high), (high, low)]
        s.partners = [(s.near, s.far), (s.far, s.near)]
        s.offset = [low * 64 + high * 32, 128 + high * 64 + low * 32]
        streams.append(s)

    axes_of_tally = ["core", "x", "y", "z"]

    def tally_send(k):
        axis = axes_of_tally[k]
        n = 2 if axis == "core" else 4
        return [
            put(tally.at[k, at[axis]], tally.at[k, at[axis]], device(at, **{axis: (at[axis] + d) % n}))
            for d in range(1, n)
        ]

    def tally_sum(k, copies):
        for copy in copies:
            copy.wait_recv()
        total = tally[k, 0]
        for slot in range(1, 2 if k == 0 else 4):
            total = total + tally[k, slot]
        return total

    tally_copies = tally_send(0)
    for s in streams:
        s.copies = [put(given[s.t].at[rows((1 - core) * half_rows, half_rows)], pair.at[s.t], device(at, core=1 - core))]
    meanwhile()
    for s in streams:
        s.copies[0].wait_recv()
        acc[s.t] = (given[s.t][rows(core * half_rows, half_rows), :] + pair[s.t]) * factor
        s.copies = []
        for u in range(2):
            away = 128 * u + (1 - s.bits[u][0]) * 64
            s.copies.append(put(acc.at[s.t, rows(away, 64)], half.at[s.t, u], device(at, **{s.axes[0]: s.partners[u][0]})))
    total = tally_sum(0, tally_copies)
    tally[1, at["x"]] = total
    tally_copies = tally_send(1)
    for s in streams:
        copies = []
        for u in range(2):
            s.copies[u].wait_recv()
            kept = rows(128 * u + s.bits[u][0] * 64, 64)
            acc[s.t, kept] = acc[s.t, kept] + half[s.t, u]
            away = 128 * u + s.bits[u][0] * 64 + (1 - s.bits[u][1]) * 32
            copies.append(put(acc.at[s.t, rows(away, 32)], quarter.at[s.t, u], device(at, **{s.axes[0]: s.partners[u][1]})))
        s.copies = copies
    total = tally_sum(1, tally_copies)
    tally[2, at["y"]] = total
    tally_copies = tally_send(2)
    for s in streams:
        q = at[s.axes[1]]
        copies = []
        for u in range(2):
            s.copies[u].wait_recv()
            kept = rows(s.offset[u], 32)
            acc[s.t, kept] = acc[s.t, kept] + quarter[s.t, u]
            for d in range(1, 4):
                to = (q + d) % 4
                copies.append(put(acc.at[s.t, rows(s.offset[u] + to * 8, 8)], two.at[s.t, q, pl.ds(u * 8, 8)],
                                  device(at, **{s.axes[1]: to})))
            two[s.t, q, u * 8 : u * 8 + 8] = acc[s.t, rows(s.offset[u] + q * 8, 8)]
        s.copies = copies
    total = tally_sum(2, tally_copies)
    tally[3, at["z"]] = total
    tally_copies = tally_send(3)
    for s in streams:
        r = at[s.axes[2]]
        for copy in s.copies:
            copy.wait_recv()
        three[s.t, r] = two[s.t, 0] + two[s.t, 1] + two[s.t, 2] + two[s.t, 3]
        s.copies = [put(three.at[s.t, r], three.at[s.t, r], device(at, **{s.axes[2]: (r + d) % 4})) for d in range(1, 4)]
    loss_out[...] = jnp.sum(tally_sum(3, tally_copies), axis=0, keepdims=True)
    base = core * half_rows
    for s in streams:
        q = at[s.axes[1]]
        for copy in s.copies:
            copy.wait_recv()
        final = three[s.t, 0] + three[s.t, 1] + three[s.t, 2] + three[s.t, 3]
        s.copies = []
        for u in range(2):
            piece = rows(base + s.offset[u] + q * 8, 8)
            outs[s.t][piece, :] = final[u * 8 : u * 8 + 8]
            for d in range(1, 4):
                s.copies.append(put(outs[s.t].at[piece], outs[s.t].at[piece], device(at, **{s.axes[1]: (q + d) % 4})))
    for s in streams:
        for copy in s.copies:
            copy.wait_recv()
        s.copies = []
        for u in range(2):
            piece = rows(base + s.offset[u], 32)
            s.copies.append(put(outs[s.t].at[piece], outs[s.t].at[piece], device(at, **{s.axes[0]: s.partners[u][1]})))
    for s in streams:
        copies = []
        for u in range(2):
            s.copies[u].wait_recv()
            piece = rows(base + 128 * u + s.bits[u][0] * 64, 64)
            copies.append(put(outs[s.t].at[piece], outs[s.t].at[piece], device(at, **{s.axes[0]: s.partners[u][0]})))
        s.copies = copies
    for s in streams:
        for copy in s.copies:
            copy.wait_recv()
        piece = rows(base, half_rows)
        s.copies = [put(outs[s.t].at[piece], outs[s.t].at[piece], device(at, core=1 - core))]
    for s in streams:
        s.copies[0].wait_recv()
    for copy in flying:
        copy.wait_send()


def step_kernel(
    x, evt, w_in, w_mid, w_out, spread, bit,
    gx_out, go_out, gm_out, gi_out, loss_out,
    fh, hid, s1, s2, ind, indp, wb, w, wn, wp, own, prev, hb, hp, nb, pb, first_col, firstp_col, entry_col,
    evp, idxn, logs, g, acc, pair, half, quarter, two, three, tally,
    small_send, small_recv, w_send, w_recv, gx_sem, send, recv, *, words, total_rows, chain,
):
    n, wide = x.shape[0], w_out.shape[1]
    parts, part = w.shape[0], w.shape[2]
    tiles, quarters = n // T, n // Q
    at = coordinates()
    me = lax.axis_index("chain")
    strata = lax.axis_index("strata")
    right, left = (strata, (me + 1) % chain), (strata, (me + chain - 1) % chain)

    barrier = pltpu.get_barrier_semaphore()
    friends = [left, right, device(at, core=1 - at["core"])]
    for axis in "xyz":
        friends += [device(at, **{axis: (at[axis] + d) % 4}) for d in range(1, 4)]
    for friend in friends:
        pl.semaphore_signal(barrier, inc=1, device_id=friend, device_id_type=MESH)
    pl.semaphore_wait(barrier, len(friends))

    def remote(source, target, s, r, to):
        return pltpu.make_async_remote_copy(
            src_ref=source, dst_ref=target, send_sem=s, recv_sem=r, device_id=to, device_id_type=MESH)

    top = words // 8 * 8
    ev_copy = remote(evt, evp, small_send.at[0], small_recv.at[0], right)
    id_copy = remote(evt.at[pl.ds(top, 8)], idxn, small_send.at[1], small_recv.at[1], left)
    ev_copy.start()
    id_copy.start()

    def to_left(c, r):
        rows = span(r, T)
        return remote(w.at[c, rows], wn.at[c, rows], w_send.at[0, c, r], w_recv.at[0, c, r], left)

    def to_right(c, r):
        rows = span(r, T)
        return remote(w.at[c, rows], wp.at[c, rows], w_send.at[1, c, r], w_recv.at[1, c, r], right)

    logs[...] = jnp.zeros_like(logs)

    def forward(r, _):
        rows = span(r, T)
        pre = dot(x[rows, :], w_in[...])
        s = sigmoid(pre)
        first = (pre * s).astype(BF16)
        fh[rows, :] = first
        s1[rows, :] = (s * (1.0 + pre * (1.0 - s))).astype(BF16)
        mid = dot(first, w_mid[...])
        s = sigmoid(mid)
        hidden = (mid * s).astype(BF16)
        hid[rows, :] = hidden
        s2[rows, :] = (s * (1.0 + mid * (1.0 - s))).astype(BF16)
        eta = dot(hidden, w_out[...])
        weight = jnp.exp(eta)
        for c in range(parts):
            w[c, rows, :] = weight[:, c * part : (c + 1) * part]
        to_left(0, r).start()
        to_right(0, r).start()
        wb[rows, :] = weight.astype(BF16)
        value = unpack(evt[:, rows], spread[...])
        flag = jnp.bitwise_and(lax.shift_right_logical(value[:, :wide], bit[...]), 1).astype(F32)
        ind[rows, :] = flag.astype(BF16)
        first_col[rows, :] = value[:, wide : wide + 128]
        entry_col[rows, :] = value[:, wide + 128 : wide + 256]
        logs[...] -= jnp.sum((flag * eta).reshape(-1, 8, wide), axis=0)
        return 0

    lax.fori_loop(0, tiles, forward, 0)

    def later(r, _):
        for c in range(1, parts):
            to_left(c, r).start()
            to_right(c, r).start()
        return 0

    lax.fori_loop(0, tiles, later, 0)

    ev_copy.wait_recv()
    id_copy.wait_recv()
    real = jnp.where(me > 0, 1.0, 0.0).astype(F32)
    idxn[...] = idxn[...] + jnp.where(me == chain - 1, 1 << 20, 0)

    def unpack_prev(r, _):
        rows = span(r, T)
        value = unpack(evp[:, rows], spread[...])
        flag = jnp.bitwise_and(lax.shift_right_logical(value[:, :wide], bit[...]), 1).astype(F32)
        indp[rows, :] = (flag * real).astype(BF16)
        firstp_col[rows, :] = value[:, wide : wide + 128]
        return 0

    lax.fori_loop(0, tiles, unpack_prev, 0)

    def lane(base):
        return lax.broadcasted_iota(I32, (Q, 128), 1) + base

    def row(table, k, j, h):
        return table[k : k + 1, j * Q + h * 128 : j * Q + (h + 1) * 128]

    FIRST, ENTRY, ENTRY_N = words, words + 1, words + 1 - top

    def own_part(i, _):
        rows = span(i, Q)
        first, firstp = first_col[rows, :], firstp_col[rows, :]
        total = totalp = 0.0
        for j in range(quarters):
            m = mask(lambda h: (row(evt, ENTRY, j, h) <= first + n) & (first <= lane(j * Q + h * 128)))
            total += dot(m, wb[j * Q : (j + 1) * Q, :])
        for c in range(parts):
            own[c, rows, :] = total[:, c * part : (c + 1) * part]
        for j in range(quarters):
            m = mask(lambda h: row(evt, ENTRY, j, h) <= firstp)
            totalp += dot(m, wb[j * Q : (j + 1) * Q, :])
        for c in range(parts):
            prev[c, rows, :] = totalp[:, c * part : (c + 1) * part]
        return 0

    lax.fori_loop(0, quarters, own_part, 0)

    eta_ref = wb
    for c in range(parts):
        cols = slice(c * part, (c + 1) * part)
        for q in range(quarters):
            for r in range(q * Q // T, (q + 1) * Q // T):
                to_left(c, r).wait_recv()
                to_right(c, r).wait_recv()
            nb[...] = wn[c, q * Q : (q + 1) * Q, :].astype(BF16)
            pb[...] = wp[c, q * Q : (q + 1) * Q, :].astype(BF16)

            def arrive(i, _):
                rows = span(i, Q)
                first, firstp = first_col[rows, :], firstp_col[rows, :]
                own[c, rows, :] += dot(mask(lambda h: row(idxn, ENTRY_N, q, h) <= first), nb[...])
                m = mask(lambda h: (row(evp, ENTRY, q, h) <= firstp + n) & (firstp <= lane(q * Q + h * 128)))
                prev[c, rows, :] += dot(m, pb[...])
                return 0

            lax.fori_loop(0, quarters, arrive, 0)

        def hazards(i, _):
            rows = span(i, T)
            divisor = own[c, rows, :]
            flag = ind[rows, cols].astype(F32) > 0.0
            hb[rows, :] = jnp.where(flag, 1.0 / divisor, 0.0).astype(BF16)
            log = jnp.where(flag, jnp.log(divisor), 0.0)
            logs[:, cols] += jnp.sum(log.reshape(-1, 8, part), axis=0)
            flagp = indp[rows, cols].astype(F32) > 0.0
            hp[rows, :] = jnp.where(flagp, 1.0 / prev[c, rows, :], 0.0).astype(BF16)
            return 0

        lax.fori_loop(0, tiles, hazards, 0)

        def expose(j, _):
            rows = span(j, Q)
            entry = entry_col[rows, :]
            here = lax.broadcasted_iota(I32, (Q, 128), 0) + j * Q
            total = 0.0
            for i in range(quarters):
                block = slice(i * Q, (i + 1) * Q)
                m = mask(lambda h: (entry <= row(evt, FIRST, i, h) + n) & (row(evt, FIRST, i, h) <= here))
                total += dot(m, hb[block, :])
                total += dot(mask(lambda h: entry <= row(evp, FIRST, i, h)), hp[block, :])
            eta_ref[rows, cols] = (w[c, rows, :] * total - ind[rows, cols].astype(F32)).astype(BF16)
            return 0

        lax.fori_loop(0, quarters, expose, 0)
        g[0, :, cols] = dot(hid[...], eta_ref[:, cols], ((0,), (0,)))

    pre_ref = s1

    def backward(i, _):
        rows = span(i, Q)
        mid_grad = (dot(eta_ref[rows, :], w_out[...], ((1,), (1,))) * s2[rows, :].astype(F32)).astype(BF16)
        pre_grad = (dot(mid_grad, w_mid[...], ((1,), (1,))) * s1[rows, :].astype(F32)).astype(BF16)
        pre_ref[rows, :] = pre_grad
        gm, gi = dot(fh[rows, :], mid_grad, ((0,), (0,))), dot(x[rows, :], pre_grad, ((0,), (0,)))

        @pl.when(i == 0)
        def _():
            g[1], g[2] = gm, gi

        @pl.when(i > 0)
        def _():
            g[1] += gm
            g[2] += gi

        return 0

    lax.fori_loop(0, quarters, backward, 0)

    tally[0, at["core"]] = logs[...] / total_rows

    def inputs_gradient():
        def tile(i, _):
            rows = span(i, Q)
            fh[rows, :] = dot(pre_ref[rows, :], w_in[...], ((1,), (1,))).astype(BF16)
            return 0

        lax.fori_loop(0, quarters, tile, 0)
        pltpu.make_async_copy(fh, gx_out, gx_sem).start()

    reduce_all([g.at[0], g.at[1], g.at[2]], total_rows ** (-0.5), [go_out, gm_out, gi_out], loss_out,
               acc, pair, half, quarter, two, three, tally, send, recv, at, inputs_gradient)
    pltpu.make_async_copy(fh, gx_out, gx_sem).wait()
    ev_copy.wait_send()
    id_copy.wait_send()

    def drain(r, _):
        for c in range(parts):
            to_left(c, r).wait_send()
            to_right(c, r).wait_send()
        return 0

    lax.fori_loop(0, tiles, drain, 0)


def on_device(features, events, tie_first, entry_row, w_in, w_mid, w_out):
    n, width = features.shape
    hidden_width, wide = w_out.shape
    words = events.shape[1]
    chain, strata = lax.axis_size("chain"), lax.axis_size("strata")
    assert (width, hidden_width, wide, n % Q) == (512, 512, 512, 0) and words % 8 in range(1, 7)
    parts = 2
    part = wide // parts
    start = lax.axis_index("chain") * n
    deep = words // 8 * 8 + 8
    evt = jnp.concatenate([
        events.T, (tie_first - start)[None], (entry_row - start + n)[None],
        jnp.zeros((deep - words - 2, n), I32)])
    column = np.arange(wide + 256)
    source = np.where(column < wide, column // WORD_BITS, words + (column - wide) // 128)
    spread = jnp.asarray((source[None, :] == np.arange(deep)[:, None]).astype(np.float32), BF16)
    bit = jnp.asarray((np.arange(wide) % WORD_BITS)[None, :].astype(np.int32))

    m = 3
    half_rows = hidden_width // 2
    messages = m * 25 + 10
    V = pltpu.VMEM
    dma = pltpu.SemaphoreType.DMA
    whole = V((n, wide), BF16)
    scratch = (
        [whole] * 7
        + [V((parts, n, part), F32)] * 5
        + [V((n, part), BF16)] * 2 + [V((Q, part), BF16)] * 2 + [V((n, 128), I32)] * 3
        + [V((deep, n), I32), V((8, n), I32), V((8, wide), F32), V((m, hidden_width, wide), F32)]
        + [V((m, half_rows, wide), F32)] * 2
        + [V((m, 2, 64, wide), F32), V((m, 2, 32, wide), F32), V((m, 4, 16, wide), F32), V((m, 4, 16, wide), F32),
           V((4, 4, 8, wide), F32)]
        + [dma((2,))] * 2 + [dma((2, parts, n // T))] * 2 + [dma, dma((messages,)), dma((messages,))]
    )
    vmem = pl.BlockSpec(memory_space=V)
    grad = jax.ShapeDtypeStruct((hidden_width, wide), F32)
    gx, go, gm, gi, loss = pl.pallas_call(
        functools.partial(step_kernel, words=words, total_rows=n * chain * strata, chain=chain),
        in_specs=[vmem] * 7,
        out_specs=[pl.BlockSpec(memory_space=pl.ANY)] + [vmem] * 4,
        out_shape=[jax.ShapeDtypeStruct((n, width), BF16), grad, grad, grad, jax.ShapeDtypeStruct((1, wide), F32)],
        scratch_shapes=scratch,
        compiler_params=pltpu.CompilerParams(
            collective_id=0, has_side_effects=True, vmem_limit_bytes=67043328),
        name="step",
    )(features, evt, w_in, w_mid, w_out, spread, bit)
    return (loss[0], gx, gi, gm, go)


def solution(mesh):
    placed = (
        P(("strata", "chain"), None),
        P(("strata", "chain"), None),
        P(("strata", "chain")),
        P(("strata", "chain")),
        P(),
        P(),
        P(),
    )
    return jax.shard_map(
        on_device,
        mesh=mesh,
        in_specs=placed,
        out_specs=(P(), P(("strata", "chain"), None), P(), P(), P()),
        check_vma=False,
    )
```

```python
import functools

import jax
import jax.numpy as jnp
import numpy as np
from jax import lax
from jax.experimental import pallas as pl
from jax.experimental.pallas import tpu as pltpu
from jax.sharding import PartitionSpec as P

T = 256
Q = 512
WORD_BITS = 15
F32 = jnp.float32
BF16 = jnp.bfloat16
I32 = jnp.int32
MESH = pl.DeviceIdType.MESH


def sigmoid(v):
    return 0.5 * jnp.tanh(0.5 * v) + 0.5


def span(i, size):
    return pl.ds(pl.multiple_of(i * size, size), size)


def dot(a, b, contract=((1,), (0,))):
    return lax.dot_general(a, b, (contract, ((), ())), preferred_element_type=F32)


def mask(build):
    return jnp.concatenate([jnp.where(build(h), 1.0, 0.0).astype(BF16) for h in range(Q // 128)], axis=1)


def unpack(words, table):
    hi = lax.shift_right_logical(words, 8).astype(F32).astype(BF16)
    lo = jnp.bitwise_and(words, 255).astype(F32).astype(BF16)
    value = dot(hi, table, ((0,), (0,))) * 256.0 + dot(lo, table, ((0,), (0,)))
    return value.astype(I32)


def coordinates():
    s, c = lax.axis_index("strata"), lax.axis_index("chain")
    return {"y": s // 2, "core": s % 2, "z": c // 4, "x": c % 4}


def device(at, **moved):
    at = {**at, **moved}
    return (at["y"] * 2 + at["core"], at["z"] * 4 + at["x"])


class Reducer:
    def __init__(self, at, factor, given, outs, acc, pair, one, red, two, three, send, recv):
        self.at, self.factor, self.given, self.outs = at, factor, given, outs
        self.acc, self.pair, self.one, self.red, self.two, self.three = acc, pair, one, red, two, three
        self.send, self.recv = send, recv
        self.count, self.flying, self.copies = 0, [], {}
        self.half = acc.shape[1]
        self.stages = [self.cores, self.first, self.second, self.third, self.back_second, self.back_first,
                       self.back_cores, self.finish]

    def put(self, source, target, **moved):
        k, self.count = self.count, self.count + 1
        copy = pltpu.make_async_remote_copy(
            src_ref=source, dst_ref=target, send_sem=self.send.at[k], recv_sem=self.recv.at[k],
            device_id=device(self.at, **moved), device_id_type=MESH,
        )
        copy.start()
        self.flying.append(copy)
        return copy

    def axis(self, t, k):
        name = "xyz"[(t + k) % 3]
        return name, self.at[name]

    def others(self, name):
        return [(self.at[name] + d) % 4 for d in range(1, 4)]

    def arrived(self, t):
        for copy in self.copies[t]:
            copy.wait_recv()

    def stage(self, k, t):
        self.stages[k](t)

    def cores(self, t):
        core = self.at["core"]
        away = span(1 - core, self.half)
        self.copies[t] = [self.put(self.given[t].at[away], self.pair.at[t], core=1 - core)]

    def first(self, t):
        name, p = self.axis(t, 0)
        self.arrived(t)
        self.acc[t] = (self.given[t][span(self.at["core"], self.half), :] + self.pair[t]) * self.factor
        size = self.half // 4
        self.copies[t] = [
            self.put(self.acc.at[t, span(to, size)], self.one.at[t, p], **{name: to}) for to in self.others(name)
        ]

    def second(self, t):
        name, p = self.axis(t, 0)
        self.arrived(t)
        total = self.acc[t, span(p, self.half // 4), :]
        for other in self.others(name):
            total = total + self.one[t, other]
        self.red[t] = total
        name, q = self.axis(t, 1)
        size = self.half // 16
        self.copies[t] = [
            self.put(self.red.at[t, span(to, size)], self.two.at[t, q], **{name: to}) for to in self.others(name)
        ]

    def third(self, t):
        name, q = self.axis(t, 1)
        self.arrived(t)
        total = self.red[t, span(q, self.half // 16), :]
        for other in self.others(name):
            total = total + self.two[t, other]
        name, r = self.axis(t, 2)
        self.three[t, r] = total
        self.copies[t] = [
            self.put(self.three.at[t, r], self.three.at[t, r], **{name: to}) for to in self.others(name)
        ]

    def rows(self, t, fine):
        p, q = self.axis(t, 0)[1], self.axis(t, 1)[1]
        block = self.at["core"] * 4 + p
        return span(block * 4 + q, self.half // 16) if fine else span(block, self.half // 4)

    def back_second(self, t):
        self.arrived(t)
        rows = self.rows(t, True)
        self.outs[t][rows, :] = self.three[t, 0] + self.three[t, 1] + self.three[t, 2] + self.three[t, 3]
        name = self.axis(t, 1)[0]
        self.copies[t] = [
            self.put(self.outs[t].at[rows], self.outs[t].at[rows], **{name: to}) for to in self.others(name)
        ]

    def back_first(self, t):
        self.arrived(t)
        rows = self.rows(t, False)
        name = self.axis(t, 0)[0]
        self.copies[t] = [
            self.put(self.outs[t].at[rows], self.outs[t].at[rows], **{name: to}) for to in self.others(name)
        ]
        self.own = getattr(self, "own", {})
        self.own[t] = self.put(self.outs[t].at[rows], self.outs[t].at[rows], core=1 - self.at["core"])

    def back_cores(self, t):
        name, p = self.axis(t, 0)
        later = [self.own[t]]
        for d, copy in enumerate(self.copies[t]):
            copy.wait_recv()
            rows = span(self.at["core"] * 4 + (p + 3 - d) % 4, self.half // 4)
            later.append(self.put(self.outs[t].at[rows], self.outs[t].at[rows], core=1 - self.at["core"]))
        self.copies[t] = later

    def finish(self, t):
        self.arrived(t)

    def drain(self):
        for copy in self.flying:
            copy.wait_send()


class Tally:
    def __init__(self, reducer, ref):
        self.reducer, self.ref, self.copies = reducer, ref, None

    def send(self, k, value):
        axis = ("core", "x", "y", "z")[k]
        at, n = self.reducer.at, 2 if k == 0 else 4
        slot = self.ref.at[k, at[axis]]
        self.ref[k, at[axis]] = value
        self.copies = [self.reducer.put(slot, slot, **{axis: (at[axis] + d) % n}) for d in range(1, n)]

    def total(self, k):
        for copy in self.copies:
            copy.wait_recv()
        total = self.ref[k, 0]
        for slot in range(1, 2 if k == 0 else 4):
            total = total + self.ref[k, slot]
        return total


def step_kernel(
    x_in, w_in_in, w_mid_in, w_out_in, events, tie, entry_in, spread, bit,
    gx_out, go_out, gm_out, gi_out, loss_out,
    x, w_in, w_mid, w_out, x_t, fh_t, hid_t, s1, s2, ind, indp, wb, w, wn, wp, own, prev, hb, hp, nb, pb,
    first_col, firstp_col, entry_col, evt, evp, idxn, logs, g, acc, pair, one, red, two, three, tally,
    in_sem, small_send, small_recv, w_send, w_recv, gx_sem, send, recv, *, words, total_rows, chain,
):
    n, wide = x.shape[0], w_out.shape[1]
    parts, part = w.shape[0], w.shape[2]
    tiles, quarters = n // T, n // Q
    at = coordinates()
    me = lax.axis_index("chain")
    strata = lax.axis_index("strata")
    right, left = (strata, (me + 1) % chain), (strata, (me + chain - 1) % chain)

    barrier = pltpu.get_barrier_semaphore()
    friends = [left, right, device(at, core=1 - at["core"])]
    for axis in "xyz":
        friends += [device(at, **{axis: (at[axis] + d) % 4}) for d in range(1, 4)]
    for friend in friends:
        pl.semaphore_signal(barrier, inc=1, device_id=friend, device_id_type=MESH)
    loads = [
        pltpu.make_async_copy(source, target, in_sem.at[k])
        for k, (source, target) in enumerate(((x_in, x), (w_in_in, w_in), (w_mid_in, w_mid), (w_out_in, w_out)))
    ]
    for load in loads:
        load.start()
    evt[0:words, :] = events[...]
    evt[words : words + 1, :] = tie[...] - me * n
    evt[words + 1 : words + 2, :] = entry_in[...] - me * n + n
    evt[words + 2 :, :] = jnp.zeros((evt.shape[0] - words - 2, n), I32)
    pl.semaphore_wait(barrier, len(friends))

    def remote(source, target, s, r, to):
        return pltpu.make_async_remote_copy(
            src_ref=source, dst_ref=target, send_sem=s, recv_sem=r, device_id=to, device_id_type=MESH)

    top = words // 8 * 8
    ev_copy = remote(evt, evp, small_send.at[0], small_recv.at[0], right)
    id_copy = remote(evt.at[pl.ds(top, 8)], idxn, small_send.at[1], small_recv.at[1], left)
    ev_copy.start()
    id_copy.start()

    def to_left(c, r):
        rows = span(r, T)
        return remote(w.at[c, rows], wn.at[c, rows], w_send.at[0, c, r], w_recv.at[0, c, r], left)

    def to_right(c, r):
        rows = span(r, T)
        return remote(w.at[c, rows], wp.at[c, rows], w_send.at[1, c, r], w_recv.at[1, c, r], right)

    logs[...] = jnp.zeros_like(logs)
    for load in loads:
        load.wait()

    def forward(r, _):
        rows = span(r, T)
        pre = dot(x[rows, :], w_in[...])
        s = sigmoid(pre)
        first = (pre * s).astype(BF16)
        s1[rows, :] = (s * (1.0 + pre * (1.0 - s))).astype(BF16)
        mid = dot(first, w_mid[...])
        s = sigmoid(mid)
        hidden = (mid * s).astype(BF16)
        s2[rows, :] = (s * (1.0 + mid * (1.0 - s))).astype(BF16)
        eta = dot(hidden, w_out[...])
        weight = jnp.exp(eta)
        for c in range(parts):
            w[c, rows, :] = weight[:, c * part : (c + 1) * part]
        to_left(0, r).start()
        to_right(0, r).start()
        wb[rows, :] = weight.astype(BF16)
        fh_t[:, rows] = first.T
        hid_t[:, rows] = hidden.T
        value = unpack(evt[:, rows], spread[...])
        flag = jnp.bitwise_and(lax.shift_right_logical(value[:, :wide], bit[...]), 1).astype(F32)
        ind[rows, :] = flag.astype(BF16)
        first_col[rows, :] = value[:, wide : wide + 128]
        entry_col[rows, :] = value[:, wide + 128 : wide + 256]
        logs[...] -= jnp.sum((flag * eta).reshape(-1, 8, wide), axis=0)
        return 0

    lax.fori_loop(0, tiles, forward, 0)

    def later(r, _):
        for c in range(1, parts):
            to_left(c, r).start()
            to_right(c, r).start()
        return 0

    lax.fori_loop(0, tiles, later, 0)

    ev_copy.wait_recv()
    id_copy.wait_recv()
    real = jnp.where(me > 0, 1.0, 0.0).astype(F32)
    idxn[...] = idxn[...] + jnp.where(me == chain - 1, 1 << 20, 0)

    def unpack_prev(r, _):
        rows = span(r, T)
        value = unpack(evp[:, rows], spread[...])
        flag = jnp.bitwise_and(lax.shift_right_logical(value[:, :wide], bit[...]), 1).astype(F32)
        indp[rows, :] = (flag * real).astype(BF16)
        firstp_col[rows, :] = value[:, wide : wide + 128]
        x_t[:, rows] = x[rows, :].T
        return 0

    lax.fori_loop(0, tiles, unpack_prev, 0)

    def lane(base):
        return lax.broadcasted_iota(I32, (Q, 128), 1) + base

    def row(table, k, j, h):
        return table[k : k + 1, j * Q + h * 128 : j * Q + (h + 1) * 128]

    FIRST, ENTRY, ENTRY_N = words, words + 1, words + 1 - top

    def own_part(i, _):
        rows = span(i, Q)
        first, firstp = first_col[rows, :], firstp_col[rows, :]
        total = totalp = 0.0
        for j in range(quarters):
            m = mask(lambda h: (row(evt, ENTRY, j, h) <= first + n) & (first <= lane(j * Q + h * 128)))
            total += dot(m, wb[j * Q : (j + 1) * Q, :])
        for c in range(parts):
            own[c, rows, :] = total[:, c * part : (c + 1) * part]
        for j in range(quarters):
            m = mask(lambda h: row(evt, ENTRY, j, h) <= firstp)
            totalp += dot(m, wb[j * Q : (j + 1) * Q, :])
        for c in range(parts):
            prev[c, rows, :] = totalp[:, c * part : (c + 1) * part]
        return 0

    lax.fori_loop(0, quarters, own_part, 0)

    def add_logs(c):
        cols = slice(c * part, (c + 1) * part)

        def tile(i, _):
            rows = span(i, T)
            log = jnp.where(ind[rows, cols].astype(F32) > 0.0, jnp.log(own[c, rows, :]), 0.0)
            logs[:, cols] += jnp.sum(log.reshape(-1, 8, part), axis=0)
            return 0

        lax.fori_loop(0, tiles, tile, 0)

    eta_ref = wb
    for c in range(parts):
        cols = slice(c * part, (c + 1) * part)
        for q in range(quarters):
            for r in range(q * Q // T, (q + 1) * Q // T):
                to_left(c, r).wait_recv()
                to_right(c, r).wait_recv()
            nb[...] = wn[c, q * Q : (q + 1) * Q, :].astype(BF16)
            pb[...] = wp[c, q * Q : (q + 1) * Q, :].astype(BF16)

            def arrive(i, _):
                rows = span(i, Q)
                first, firstp = first_col[rows, :], firstp_col[rows, :]
                own[c, rows, :] += dot(mask(lambda h: row(idxn, ENTRY_N, q, h) <= first), nb[...])
                m = mask(lambda h: (row(evp, ENTRY, q, h) <= firstp + n) & (firstp <= lane(q * Q + h * 128)))
                prev[c, rows, :] += dot(m, pb[...])
                return 0

            lax.fori_loop(0, quarters, arrive, 0)

        def hazards(i, _):
            rows = span(i, T)
            divisor = own[c, rows, :]
            flag = ind[rows, cols].astype(F32) > 0.0
            hb[rows, :] = jnp.where(flag, 1.0 / divisor, 0.0).astype(BF16)
            flagp = indp[rows, cols].astype(F32) > 0.0
            hp[rows, :] = jnp.where(flagp, 1.0 / prev[c, rows, :], 0.0).astype(BF16)
            return 0

        lax.fori_loop(0, tiles, hazards, 0)

        def expose(j, _):
            rows = span(j, Q)
            entry = entry_col[rows, :]
            here = lax.broadcasted_iota(I32, (Q, 128), 0) + j * Q
            total = 0.0
            for i in range(quarters):
                block = slice(i * Q, (i + 1) * Q)
                m = mask(lambda h: (entry <= row(evt, FIRST, i, h) + n) & (row(evt, FIRST, i, h) <= here))
                total += dot(m, hb[block, :])
                total += dot(mask(lambda h: entry <= row(evp, FIRST, i, h)), hp[block, :])
            eta_ref[rows, cols] = (w[c, rows, :] * total - ind[rows, cols].astype(F32)).astype(BF16)
            return 0

        lax.fori_loop(0, quarters, expose, 0)
        g[0, :, cols] = dot(hid_t[...], eta_ref[:, cols])
        if c < parts - 1:
            add_logs(c)

    mid_ref, pre_ref, gx = s2, s1, x
    reducer = Reducer(at, total_rows ** (-0.5), [g.at[t] for t in range(3)], [go_out, gm_out, gi_out],
                      acc, pair, one, red, two, three, send, recv)
    counted = Tally(reducer, tally)

    def turn(k):
        for t in range(2, -1, -1):
            if 0 <= k - t < len(reducer.stages):
                reducer.stage(k - t, t)

    turn(0)

    def middle(i, _):
        rows = span(i, Q)
        mid_grad = dot(eta_ref[rows, :], w_out[...], ((1,), (1,))) * s2[rows, :].astype(F32)
        mid_ref[rows, :] = mid_grad.astype(BF16)
        return 0

    lax.fori_loop(0, quarters, middle, 0)
    g[1] = dot(fh_t[...], mid_ref[...])
    turn(1)

    def inner(i, _):
        rows = span(i, Q)
        pre_grad = dot(mid_ref[rows, :], w_mid[...], ((1,), (1,))) * s1[rows, :].astype(F32)
        pre_ref[rows, :] = pre_grad.astype(BF16)
        return 0

    lax.fori_loop(0, quarters, inner, 0)
    g[2] = dot(x_t[...], pre_ref[...])
    turn(2)
    add_logs(parts - 1)
    counted.send(0, logs[...] / total_rows)

    def last(i, _):
        rows = span(i, Q)
        gx[rows, :] = dot(pre_ref[rows, :], w_in[...], ((1,), (1,))).astype(BF16)
        return 0

    turn(3)
    counted.send(1, counted.total(0))
    lax.fori_loop(0, quarters, last, 0)
    gx_copy = pltpu.make_async_copy(gx, gx_out, gx_sem)
    gx_copy.start()
    turn(4)
    counted.send(2, counted.total(1))
    turn(5)
    counted.send(3, counted.total(2))
    turn(6)
    loss_out[...] = jnp.sum(counted.total(3), axis=0, keepdims=True)
    for k in range(7, len(reducer.stages) + 2):
        turn(k)
    reducer.drain()
    gx_copy.wait()
    ev_copy.wait_send()
    id_copy.wait_send()

    def drain(r, _):
        for c in range(parts):
            to_left(c, r).wait_send()
            to_right(c, r).wait_send()
        return 0

    lax.fori_loop(0, tiles, drain, 0)


def copy_kernel(*refs):
    m = len(refs) // 2
    for source, target in zip(refs[:m], refs[m:]):
        target[...] = source[...]


def on_device(features, events, tie_first, entry_row, w_in, w_mid, w_out):
    n, width = features.shape
    hidden_width, wide = w_out.shape
    words = events.shape[1]
    chain, strata = lax.axis_size("chain"), lax.axis_size("strata")
    assert (width, hidden_width, wide, n % Q) == (512, 512, 512, 0) and words % 8 in range(1, 7)
    parts = 2
    part = wide // parts
    deep = words // 8 * 8 + 8
    column = np.arange(wide + 256)
    source = np.where(column < wide, column // WORD_BITS, words + (column - wide) // 128)
    spread = jnp.asarray((source[None, :] == np.arange(deep)[:, None]).astype(np.float32), BF16)
    bit = jnp.asarray((np.arange(wide) % WORD_BITS)[None, :].astype(np.int32))

    m = 3
    half = hidden_width // 2
    messages = m * 20 + 10
    V = pltpu.VMEM
    dma = pltpu.SemaphoreType.DMA
    by_rows, by_columns, square = V((n, wide), BF16), V((wide, n), BF16), V((wide, wide), BF16)
    scratch = (
        [by_rows] + [square] * 3 + [by_columns] * 3 + [by_rows] * 5
        + [V((parts, n, part), F32)] * 5
        + [V((n, part), BF16)] * 2 + [V((Q, part), BF16)] * 2 + [V((n, 128), I32)] * 3
        + [V((deep, n), I32)] * 2 + [V((8, n), I32), V((8, wide), F32), V((m, hidden_width, wide), F32)]
        + [V((m, half, wide), F32)] * 2
        + [V((m, 4, half // 4, wide), F32), V((m, half // 4, wide), F32)]
        + [V((m, 4, half // 16, wide), F32)] * 2 + [V((4, 4, 8, wide), F32)]
        + [dma((4,))] + [dma((2,))] * 2 + [dma((2, parts, n // T))] * 2 + [dma, dma((messages,)), dma((messages,))]
    )
    vmem = pl.BlockSpec(memory_space=V)
    anywhere = pl.BlockSpec(memory_space=pl.ANY)
    grad = jax.ShapeDtypeStruct((hidden_width, wide), F32)
    shapes = [jax.ShapeDtypeStruct((n, width), BF16), grad, grad, grad, jax.ShapeDtypeStruct((1, wide), F32)]
    results = pl.pallas_call(
        functools.partial(step_kernel, words=words, total_rows=n * chain * strata, chain=chain),
        in_specs=[anywhere] * 4 + [vmem] * 5,
        out_specs=[anywhere] + [vmem] * 4,
        out_shape=shapes,
        scratch_shapes=scratch,
        compiler_params=pltpu.CompilerParams(
            collective_id=0, has_side_effects=True, vmem_limit_bytes=67043328),
        name="step",
    )(features, w_in, w_mid, w_out, events.T, tie_first[None], entry_row[None], spread, bit)
    steps = 4
    blocks = [pl.BlockSpec((r.shape[0] // steps, r.shape[1]), lambda i: (i, 0)) for r in shapes[:4]]
    blocks.append(pl.BlockSpec(shapes[4].shape, lambda i: (0, 0)))
    gx, go, gm, gi, loss = pl.pallas_call(
        copy_kernel, grid=(steps,), in_specs=blocks, out_specs=blocks, out_shape=shapes, name="results",
    )(*results)
    return (loss[0], gx, gi, gm, go)


def solution(mesh):
    placed = (
        P(("strata", "chain"), None),
        P(("strata", "chain"), None),
        P(("strata", "chain")),
        P(("strata", "chain")),
        P(),
        P(),
        P(),
    )
    return jax.shard_map(
        on_device,
        mesh=mesh,
        in_specs=placed,
        out_specs=(P(), P(("strata", "chain"), None), P(), P(), P()),
        check_vma=False,
    )
```

```python
import functools

import jax
import jax.numpy as jnp
import numpy as np
from jax import lax
from jax.experimental import pallas as pl
from jax.experimental.pallas import tpu as pltpu
from jax.sharding import PartitionSpec as P

T = 256
Q = 512
WORD_BITS = 15
F32 = jnp.float32
BF16 = jnp.bfloat16
I32 = jnp.int32
MESH = pl.DeviceIdType.MESH


def sigmoid(v):
    return 0.5 * jnp.tanh(0.5 * v) + 0.5


def span(i, size):
    return pl.ds(pl.multiple_of(i * size, size), size)


def dot(a, b, contract=((1,), (0,))):
    return lax.dot_general(a, b, (contract, ((), ())), preferred_element_type=F32)


def mask(build):
    return jnp.concatenate([jnp.where(build(h), 1.0, 0.0).astype(BF16) for h in range(Q // 128)], axis=1)


def unpack(words, table):
    hi = lax.shift_right_logical(words, 8).astype(F32).astype(BF16)
    lo = jnp.bitwise_and(words, 255).astype(F32).astype(BF16)
    value = dot(hi, table, ((0,), (0,))) * 256.0 + dot(lo, table, ((0,), (0,)))
    return value.astype(I32)


def coordinates():
    s, c = lax.axis_index("strata"), lax.axis_index("chain")
    return {"y": s // 2, "core": s % 2, "z": c // 4, "x": c % 4}


def device(at, **moved):
    at = {**at, **moved}
    return (at["y"] * 2 + at["core"], at["z"] * 4 + at["x"])


class Reducer:
    def __init__(self, at, factor, given, outs, acc, pair, one, red, two, three, send, recv):
        self.at, self.factor, self.given, self.outs = at, factor, given, outs
        self.acc, self.pair, self.one, self.red, self.two, self.three = acc, pair, one, red, two, three
        self.send, self.recv = send, recv
        self.count, self.flying, self.copies, self.own = 0, [], {}, {}
        self.block, self.per = acc.shape[1], acc.shape[0] // len(given)
        self.stages = [self.cores, self.first, self.second, self.third, self.back_second, self.back_first,
                       self.back_cores, self.finish]

    def put(self, source, target, **moved):
        k, self.count = self.count, self.count + 1
        copy = pltpu.make_async_remote_copy(
            src_ref=source, dst_ref=target, send_sem=self.send.at[k], recv_sem=self.recv.at[k],
            device_id=device(self.at, **moved), device_id_type=MESH,
        )
        copy.start()
        self.flying.append(copy)
        return copy

    def axis(self, t, k):
        name = "xyz"[(t + k) % 3]
        return name, self.at[name]

    def others(self, name):
        return [(self.at[name] + d) % 4 for d in (2, 1, 3)]

    def rows_of(self, t, core, start, size):
        blocks = self.block // size
        return span((core * self.per + t % self.per) * blocks + start, size)

    def arrived(self, t):
        for copy in self.copies[t]:
            copy.wait_recv()

    def stage(self, k, t):
        self.stages[k](t)

    def cores(self, t):
        core = self.at["core"]
        away = self.rows_of(t, 1 - core, 0, self.block)
        self.copies[t] = [self.put(self.given[t // self.per].at[away], self.pair.at[t], core=1 - core)]

    def first(self, t):
        name, p = self.axis(t, 0)
        self.arrived(t)
        kept = self.rows_of(t, self.at["core"], 0, self.block)
        self.acc[t] = (self.given[t // self.per][kept, :] + self.pair[t]) * self.factor
        size = self.block // 4
        self.copies[t] = [
            self.put(self.acc.at[t, span(to, size)], self.one.at[t, p], **{name: to}) for to in self.others(name)
        ]

    def second(self, t):
        name, p = self.axis(t, 0)
        self.arrived(t)
        total = self.acc[t, span(p, self.block // 4), :]
        for other in self.others(name):
            total = total + self.one[t, other]
        self.red[t] = total
        name, q = self.axis(t, 1)
        size = self.block // 16
        self.copies[t] = [
            self.put(self.red.at[t, span(to, size)], self.two.at[t, q], **{name: to}) for to in self.others(name)
        ]

    def third(self, t):
        name, q = self.axis(t, 1)
        self.arrived(t)
        total = self.red[t, span(q, self.block // 16), :]
        for other in self.others(name):
            total = total + self.two[t, other]
        name, r = self.axis(t, 2)
        self.three[t, r] = total
        self.copies[t] = [
            self.put(self.three.at[t, r], self.three.at[t, r], **{name: to}) for to in self.others(name)
        ]

    def rows(self, t, fine):
        p, q = self.axis(t, 0)[1], self.axis(t, 1)[1]
        core = self.at["core"]
        return self.rows_of(t, core, p * 4 + q, self.block // 16) if fine else self.rows_of(t, core, p, self.block // 4)

    def spread(self, t, rows, name):
        piece = self.outs[t // self.per].at[rows]
        return [self.put(piece, piece, **{name: to}) for to in self.others(name)]

    def back_second(self, t):
        self.arrived(t)
        rows = self.rows(t, True)
        total = self.three[t, 0] + self.three[t, 1] + self.three[t, 2] + self.three[t, 3]
        self.outs[t // self.per][rows, :] = total
        self.copies[t] = self.spread(t, rows, self.axis(t, 1)[0])

    def back_first(self, t):
        self.arrived(t)
        rows = self.rows(t, False)
        self.copies[t] = self.spread(t, rows, self.axis(t, 0)[0])
        piece = self.outs[t // self.per].at[rows]
        self.own[t] = self.put(piece, piece, core=1 - self.at["core"])

    def back_cores(self, t):
        p = self.axis(t, 0)[1]
        later = [self.own[t]]
        for d, copy in zip((2, 1, 3), self.copies[t]):
            copy.wait_recv()
            rows = self.rows_of(t, self.at["core"], (p + 4 - d) % 4, self.block // 4)
            piece = self.outs[t // self.per].at[rows]
            later.append(self.put(piece, piece, core=1 - self.at["core"]))
        self.copies[t] = later

    def finish(self, t):
        self.arrived(t)

    def drain(self):
        for copy in self.flying:
            copy.wait_send()


class Tally:
    def __init__(self, reducer, ref):
        self.reducer, self.ref, self.copies = reducer, ref, None

    def send(self, k, value):
        axis = ("core", "x", "y", "z")[k]
        at, n = self.reducer.at, 2 if k == 0 else 4
        slot = self.ref.at[k, at[axis]]
        self.ref[k, at[axis]] = value
        self.copies = [self.reducer.put(slot, slot, **{axis: (at[axis] + d) % n}) for d in range(1, n)]

    def total(self, k):
        for copy in self.copies:
            copy.wait_recv()
        total = self.ref[k, 0]
        for slot in range(1, 2 if k == 0 else 4):
            total = total + self.ref[k, slot]
        return total


def step_kernel(
    x_in, w_in_in, w_mid_in, w_out_in, events, tie, entry_in, spread, bit,
    gx_out, go_out, gm_out, gi_out, loss_out,
    sums, x, w_in, w_mid, w_out, x_t, fh_t, hid_t, s1, s2, ind, indp, wb, w, wn, wp, own, prev, hb, hp, nb, pb,
    first_col, firstp_col, entry_col, evt, evp, idxn, logs, g, acc, pair, one, red, two, three, tally,
    in_sem, out_sem, small_send, small_recv, w_send, w_recv, gx_sem, send, recv, *, words, total_rows, chain,
):
    n, wide = x.shape[0], w_out.shape[1]
    parts, part = w.shape[0], w.shape[2]
    tiles, quarters = n // T, n // Q
    at = coordinates()
    me = lax.axis_index("chain")
    strata = lax.axis_index("strata")
    right, left = (strata, (me + 1) % chain), (strata, (me + chain - 1) % chain)

    barrier = pltpu.get_barrier_semaphore()
    friends = [left, right, device(at, core=1 - at["core"])]
    for axis in "xyz":
        friends += [device(at, **{axis: (at[axis] + d) % 4}) for d in range(1, 4)]
    for friend in friends:
        pl.semaphore_signal(barrier, inc=1, device_id=friend, device_id_type=MESH)
    loads = [
        pltpu.make_async_copy(source, target, in_sem.at[k])
        for k, (source, target) in enumerate(((x_in, x), (w_in_in, w_in), (w_mid_in, w_mid), (w_out_in, w_out)))
    ]
    for load in loads:
        load.start()
    evt[0:words, :] = events[...]
    evt[words : words + 1, :] = tie[...] - me * n
    evt[words + 1 : words + 2, :] = entry_in[...] - me * n + n
    evt[words + 2 :, :] = jnp.zeros((evt.shape[0] - words - 2, n), I32)
    pl.semaphore_wait(barrier, len(friends))

    def remote(source, target, s, r, to):
        return pltpu.make_async_remote_copy(
            src_ref=source, dst_ref=target, send_sem=s, recv_sem=r, device_id=to, device_id_type=MESH)

    top = words // 8 * 8
    ev_copy = remote(evt, evp, small_send.at[0], small_recv.at[0], right)
    id_copy = remote(evt.at[pl.ds(top, 8)], idxn, small_send.at[1], small_recv.at[1], left)
    ev_copy.start()
    id_copy.start()

    def to_left(c, r):
        rows = span(r, T)
        return remote(w.at[c, rows], wn.at[c, rows], w_send.at[0, c, r], w_recv.at[0, c, r], left)

    def to_right(c, r):
        rows = span(r, T)
        return remote(w.at[c, rows], wp.at[c, rows], w_send.at[1, c, r], w_recv.at[1, c, r], right)

    logs[...] = jnp.zeros_like(logs)
    for load in loads:
        load.wait()

    def forward(r, _):
        rows = span(r, T)
        pre = dot(x[rows, :], w_in[...])
        s = sigmoid(pre)
        first = (pre * s).astype(BF16)
        s1[rows, :] = (s * (1.0 + pre * (1.0 - s))).astype(BF16)
        mid = dot(first, w_mid[...])
        s = sigmoid(mid)
        hidden = (mid * s).astype(BF16)
        s2[rows, :] = (s * (1.0 + mid * (1.0 - s))).astype(BF16)
        eta = dot(hidden, w_out[...])
        weight = jnp.exp(eta)
        for c in range(parts):
            w[c, rows, :] = weight[:, c * part : (c + 1) * part]
        to_left(0, r).start()
        to_right(0, r).start()
        wb[rows, :] = weight.astype(BF16)
        fh_t[:, rows] = first.T
        hid_t[:, rows] = hidden.T
        value = unpack(evt[:, rows], spread[...])
        flag = jnp.bitwise_and(lax.shift_right_logical(value[:, :wide], bit[...]), 1).astype(F32)
        ind[rows, :] = flag.astype(BF16)
        first_col[rows, :] = value[:, wide : wide + 128]
        entry_col[rows, :] = value[:, wide + 128 : wide + 256]
        logs[...] -= jnp.sum((flag * eta).reshape(-1, 8, wide), axis=0)
        return 0

    lax.fori_loop(0, tiles, forward, 0)

    def later(r, _):
        for c in range(1, parts):
            to_left(c, r).start()
            to_right(c, r).start()
        return 0

    lax.fori_loop(0, tiles, later, 0)

    ev_copy.wait_recv()
    id_copy.wait_recv()
    real = jnp.where(me > 0, 1.0, 0.0).astype(F32)
    idxn[...] = idxn[...] + jnp.where(me == chain - 1, 1 << 20, 0)

    def unpack_prev(r, _):
        rows = span(r, T)
        value = unpack(evp[:, rows], spread[...])
        flag = jnp.bitwise_and(lax.shift_right_logical(value[:, :wide], bit[...]), 1).astype(F32)
        indp[rows, :] = (flag * real).astype(BF16)
        firstp_col[rows, :] = value[:, wide : wide + 128]
        x_t[:, rows] = x[rows, :].T
        return 0

    lax.fori_loop(0, tiles, unpack_prev, 0)

    def lane(base):
        return lax.broadcasted_iota(I32, (Q, 128), 1) + base

    def row(table, k, j, h):
        return table[k : k + 1, j * Q + h * 128 : j * Q + (h + 1) * 128]

    FIRST, ENTRY, ENTRY_N = words, words + 1, words + 1 - top

    def own_part(i, _):
        rows = span(i, Q)
        first, firstp = first_col[rows, :], firstp_col[rows, :]
        total = totalp = 0.0
        for j in range(quarters):
            m = mask(lambda h: (row(evt, ENTRY, j, h) <= first + n) & (first <= lane(j * Q + h * 128)))
            total += dot(m, wb[j * Q : (j + 1) * Q, :])
        for c in range(parts):
            own[c, rows, :] = total[:, c * part : (c + 1) * part]
        for j in range(quarters):
            m = mask(lambda h: row(evt, ENTRY, j, h) <= firstp)
            totalp += dot(m, wb[j * Q : (j + 1) * Q, :])
        for c in range(parts):
            prev[c, rows, :] = totalp[:, c * part : (c + 1) * part]
        return 0

    lax.fori_loop(0, quarters, own_part, 0)

    def add_logs(c):
        cols = slice(c * part, (c + 1) * part)

        def tile(i, _):
            rows = span(i, T)
            log = jnp.where(ind[rows, cols].astype(F32) > 0.0, jnp.log(own[c, rows, :]), 0.0)
            logs[:, cols] += jnp.sum(log.reshape(-1, 8, part), axis=0)
            return 0

        lax.fori_loop(0, tiles, tile, 0)

    eta_ref = wb

    def from_next(c, q):
        for r in range(q * Q // T, (q + 1) * Q // T):
            to_left(c, r).wait_recv()
        nb[...] = wn[c, q * Q : (q + 1) * Q, :].astype(BF16)

        def tile(i, _):
            rows = span(i, Q)
            first = first_col[rows, :]
            own[c, rows, :] += dot(mask(lambda h: row(idxn, ENTRY_N, q, h) <= first), nb[...])
            return 0

        lax.fori_loop(0, quarters, tile, 0)

    def from_previous(c, q):
        for r in range(q * Q // T, (q + 1) * Q // T):
            to_right(c, r).wait_recv()
        pb[...] = wp[c, q * Q : (q + 1) * Q, :].astype(BF16)

        def tile(i, _):
            rows = span(i, Q)
            firstp = firstp_col[rows, :]
            m = mask(lambda h: (row(evp, ENTRY, q, h) <= firstp + n) & (firstp <= lane(q * Q + h * 128)))
            prev[c, rows, :] += dot(m, pb[...])
            return 0

        lax.fori_loop(0, quarters, tile, 0)

    def hazards(flags, divisors, target):
        def tile(i, _):
            rows = span(i, T)
            flag = flags(rows).astype(F32) > 0.0
            target[rows, :] = jnp.where(flag, 1.0 / divisors(rows), 0.0).astype(BF16)
            return 0

        lax.fori_loop(0, tiles, tile, 0)

    for c in range(parts):
        cols = slice(c * part, (c + 1) * part)
        for q in range(quarters):
            from_next(c, q)
            if q < quarters - 1:
                from_previous(c, q)
        hazards(lambda rows: ind[rows, cols], lambda rows: own[c, rows, :], hb)

        def expose_own(j, _):
            rows = span(j, Q)
            entry = entry_col[rows, :]
            here = lax.broadcasted_iota(I32, (Q, 128), 0) + j * Q
            total = 0.0
            for i in range(quarters):
                m = mask(lambda h: (entry <= row(evt, FIRST, i, h) + n) & (row(evt, FIRST, i, h) <= here))
                total += dot(m, hb[i * Q : (i + 1) * Q, :])
            wn[c, rows, :] = total
            return 0

        lax.fori_loop(0, quarters, expose_own, 0)
        from_previous(c, quarters - 1)
        hazards(lambda rows: indp[rows, cols], lambda rows: prev[c, rows, :], hp)

        def expose(j, _):
            rows = span(j, Q)
            entry = entry_col[rows, :]
            total = wn[c, rows, :]
            for i in range(quarters):
                total += dot(mask(lambda h: entry <= row(evp, FIRST, i, h)), hp[i * Q : (i + 1) * Q, :])
            eta_ref[rows, cols] = (w[c, rows, :] * total - ind[rows, cols].astype(F32)).astype(BF16)
            return 0

        lax.fori_loop(0, quarters, expose, 0)
        g[0, :, cols] = dot(hid_t[...], eta_ref[:, cols])
        if c < parts - 1:
            add_logs(c)

    mid_ref, pre_ref, gx = s2, s1, x
    reducer = Reducer(at, total_rows ** (-0.5), [g.at[t] for t in range(3)], [sums.at[t] for t in range(3)],
                      acc, pair, one, red, two, three, send, recv)
    counted = Tally(reducer, tally)

    outs = [pltpu.make_async_copy(sums.at[t], out, out_sem.at[t]) for t, out in enumerate((go_out, gm_out, gi_out))]

    def turn(k):
        for t in range(2, -1, -1):
            if 0 <= k - t < len(reducer.stages):
                for v in range(reducer.per):
                    reducer.stage(k - t, t * reducer.per + v)
                if k - t == len(reducer.stages) - 1:
                    outs[t].start()

    turn(0)

    def middle(i, _):
        rows = span(i, Q)
        mid_grad = dot(eta_ref[rows, :], w_out[...], ((1,), (1,))) * s2[rows, :].astype(F32)
        mid_ref[rows, :] = mid_grad.astype(BF16)
        return 0

    lax.fori_loop(0, quarters, middle, 0)
    g[1] = dot(fh_t[...], mid_ref[...])
    turn(1)

    def inner(i, _):
        rows = span(i, Q)
        pre_grad = dot(mid_ref[rows, :], w_mid[...], ((1,), (1,))) * s1[rows, :].astype(F32)
        pre_ref[rows, :] = pre_grad.astype(BF16)
        return 0

    lax.fori_loop(0, quarters, inner, 0)
    g[2] = dot(x_t[...], pre_ref[...])
    turn(2)
    add_logs(parts - 1)
    counted.send(0, logs[...] / total_rows)

    def last(i, _):
        rows = span(i, Q)
        gx[rows, :] = dot(pre_ref[rows, :], w_in[...], ((1,), (1,))).astype(BF16)
        return 0

    turn(3)
    counted.send(1, counted.total(0))
    lax.fori_loop(0, quarters, last, 0)
    gx_copy = pltpu.make_async_copy(gx, gx_out, gx_sem)
    gx_copy.start()
    turn(4)
    counted.send(2, counted.total(1))
    turn(5)
    counted.send(3, counted.total(2))
    turn(6)
    loss_out[...] = jnp.sum(counted.total(3), axis=0, keepdims=True)
    for k in range(7, len(reducer.stages) + 2):
        turn(k)
    reducer.drain()
    gx_copy.wait()
    for out in outs:
        out.wait()
    ev_copy.wait_send()
    id_copy.wait_send()

    def drain(r, _):
        for c in range(parts):
            to_left(c, r).wait_send()
            to_right(c, r).wait_send()
        return 0

    lax.fori_loop(0, tiles, drain, 0)


def copy_kernel(*refs):
    m = (len(refs) - 2) // 3
    sources, targets, buffers, sem_in, sem_out = refs[:m], refs[m : 2 * m], refs[2 * m : 3 * m], refs[-2], refs[-1]
    reads, writes = [], []
    for source, target, buffer in zip(sources, targets, buffers):
        pieces = max(source.shape[0] // 256, 1) if source.dtype == F32 else source.shape[0] // 512
        size = source.shape[0] // pieces
        for k in range(pieces):
            at = pl.ds(k * size, size)
            i = len(reads)
            reads.append(pltpu.make_async_copy(source.at[at], buffer.at[at], sem_in.at[i]))
            writes.append(pltpu.make_async_copy(buffer.at[at], target.at[at], sem_out.at[i]))
    for read in reads:
        read.start()
    for read, write in zip(reads, writes):
        read.wait()
        write.start()
    for write in writes:
        write.wait()


def on_device(features, events, tie_first, entry_row, w_in, w_mid, w_out):
    n, width = features.shape
    hidden_width, wide = w_out.shape
    words = events.shape[1]
    chain, strata = lax.axis_size("chain"), lax.axis_size("strata")
    assert (width, hidden_width, wide, n % Q) == (512, 512, 512, 0) and words % 8 in range(1, 7)
    parts = 2
    part = wide // parts
    deep = words // 8 * 8 + 8
    column = np.arange(wide + 256)
    source = np.where(column < wide, column // WORD_BITS, words + (column - wide) // 128)
    spread = jnp.asarray((source[None, :] == np.arange(deep)[:, None]).astype(np.float32), BF16)
    bit = jnp.asarray((np.arange(wide) % WORD_BITS)[None, :].astype(np.int32))

    m = 3
    per = 2
    streams, block = m * per, hidden_width // 2 // per
    messages = streams * 20 + 10
    V = pltpu.VMEM
    dma = pltpu.SemaphoreType.DMA
    by_rows, by_columns, square = V((n, wide), BF16), V((wide, n), BF16), V((wide, wide), BF16)
    scratch = (
        [V((m, hidden_width, wide), F32), by_rows] + [square] * 3 + [by_columns] * 3 + [by_rows] * 5
        + [V((parts, n, part), F32)] * 5
        + [V((n, part), BF16)] * 2 + [V((Q, part), BF16)] * 2 + [V((n, 128), I32)] * 3
        + [V((deep, n), I32)] * 2 + [V((8, n), I32), V((8, wide), F32), V((m, hidden_width, wide), F32)]
        + [V((streams, block, wide), F32)] * 2
        + [V((streams, 4, block // 4, wide), F32), V((streams, block // 4, wide), F32)]
        + [V((streams, 4, block // 16, wide), F32)] * 2 + [V((4, 4, 8, wide), F32)]
        + [dma((4,)), dma((m,))] + [dma((2,))] * 2 + [dma((2, parts, n // T))] * 2 + [dma, dma((messages,)), dma((messages,))]
    )
    vmem = pl.BlockSpec(memory_space=V)
    anywhere = pl.BlockSpec(memory_space=pl.ANY)
    grad = jax.ShapeDtypeStruct((hidden_width, wide), F32)
    shapes = [jax.ShapeDtypeStruct((n, width), BF16), grad, grad, grad, jax.ShapeDtypeStruct((1, wide), F32)]
    results = pl.pallas_call(
        functools.partial(step_kernel, words=words, total_rows=n * chain * strata, chain=chain),
        in_specs=[anywhere] * 4 + [vmem] * 5,
        out_specs=[anywhere] * 4 + [vmem],
        out_shape=shapes,
        scratch_shapes=scratch,
        compiler_params=pltpu.CompilerParams(
            collective_id=0, has_side_effects=True, vmem_limit_bytes=67043328),
        name="step",
    )(features, w_in, w_mid, w_out, events.T, tie_first[None], entry_row[None], spread, bit)
    gx, go, gm, gi, loss = pl.pallas_call(
        copy_kernel,
        in_specs=[anywhere] * 5,
        out_specs=[anywhere] * 5,
        out_shape=shapes,
        scratch_shapes=[V(shape.shape, shape.dtype) for shape in shapes] + [dma((16,))] * 2,
        name="results",
    )(*results)
    return (loss[0], gx, gi, gm, go)


def solution(mesh):
    placed = (
        P(("strata", "chain"), None),
        P(("strata", "chain"), None),
        P(("strata", "chain")),
        P(("strata", "chain")),
        P(),
        P(),
        P(),
    )
    return jax.shard_map(
        on_device,
        mesh=mesh,
        in_specs=placed,
        out_specs=(P(), P(("strata", "chain"), None), P(), P(), P()),
        check_vma=False,
    )
```

```python
import functools

import jax
import jax.numpy as jnp
import numpy as np
from jax import lax
from jax.experimental import pallas as pl
from jax.experimental.pallas import tpu as pltpu
from jax.sharding import PartitionSpec as P

T = 256
Q = 512
WORD_BITS = 15
F32 = jnp.float32
BF16 = jnp.bfloat16
I32 = jnp.int32
MESH = pl.DeviceIdType.MESH


def sigmoid(v):
    return 0.5 * jnp.tanh(0.5 * v) + 0.5


def span(i, size):
    return pl.ds(pl.multiple_of(i * size, size), size)


def dot(a, b, contract=((1,), (0,))):
    return lax.dot_general(a, b, (contract, ((), ())), preferred_element_type=F32)


def mask(build):
    return jnp.concatenate([jnp.where(build(h), 1.0, 0.0).astype(BF16) for h in range(Q // 128)], axis=1)


def unpack(words, table):
    hi = lax.shift_right_logical(words, 8).astype(F32).astype(BF16)
    lo = jnp.bitwise_and(words, 255).astype(F32).astype(BF16)
    value = dot(hi, table, ((0,), (0,))) * 256.0 + dot(lo, table, ((0,), (0,)))
    return value.astype(I32)


def coordinates():
    s, c = lax.axis_index("strata"), lax.axis_index("chain")
    return {"y": s // 2, "core": s % 2, "z": c // 4, "x": c % 4}


def device(at, **moved):
    at = {**at, **moved}
    return (at["y"] * 2 + at["core"], at["z"] * 4 + at["x"])


class Reducer:
    def __init__(self, at, factor, streams, given, outs, acc, pair, one, red, two, three, send, recv):
        self.at, self.factor, self.streams, self.given, self.outs = at, factor, streams, given, outs
        self.acc, self.pair, self.one, self.red, self.two, self.three = acc, pair, one, red, two, three
        self.send, self.recv = send, recv
        self.count, self.flying, self.copies, self.own = 0, [], {}, {}
        self.half = given[0].shape[0] // 2
        self.stages = [self.cores, self.first, self.second, self.third, self.back_second, self.back_first,
                       self.back_cores, self.finish]

    def put(self, source, target, **moved):
        k, self.count = self.count, self.count + 1
        copy = pltpu.make_async_remote_copy(
            src_ref=source, dst_ref=target, send_sem=self.send.at[k], recv_sem=self.recv.at[k],
            device_id=device(self.at, **moved), device_id_type=MESH,
        )
        copy.start()
        self.flying.append(copy)
        return copy

    def matrix(self, t):
        return self.streams[t][0]

    def size(self, t, cut=1):
        return self.streams[t][2] // cut

    def axis(self, t, k):
        name = "xyz"[(self.streams[t][3] + k) % 3]
        return name, self.at[name]

    def others(self, name):
        return [(self.at[name] + d) % 4 for d in (2, 1, 3)]

    def rows_of(self, t, core, start, size):
        return span(core * (self.half // size) + self.streams[t][1] // size + start, size)

    def arrived(self, t):
        for copy in self.copies[t]:
            copy.wait_recv()

    def cores(self, t):
        core, size = self.at["core"], self.size(t)
        away = self.rows_of(t, 1 - core, 0, size)
        self.copies[t] = [
            self.put(self.given[self.matrix(t)].at[away], self.pair.at[t, pl.ds(0, size)], core=1 - core)
        ]

    def first(self, t):
        name, p = self.axis(t, 0)
        self.arrived(t)
        size = self.size(t)
        kept = self.rows_of(t, self.at["core"], 0, size)
        self.acc[t, 0:size, :] = (self.given[self.matrix(t)][kept, :] + self.pair[t, 0:size, :]) * self.factor
        size = self.size(t, 4)
        self.copies[t] = [
            self.put(self.acc.at[t, span(to, size)], self.one.at[t, p, pl.ds(0, size)], **{name: to})
            for to in self.others(name)
        ]

    def second(self, t):
        name, p = self.axis(t, 0)
        self.arrived(t)
        size = self.size(t, 4)
        total = self.acc[t, span(p, size), :]
        for other in self.others(name):
            total = total + self.one[t, other, 0:size, :]
        self.red[t, 0:size, :] = total
        name, q = self.axis(t, 1)
        size = self.size(t, 16)
        self.copies[t] = [
            self.put(self.red.at[t, span(to, size)], self.two.at[t, q, pl.ds(0, size)], **{name: to})
            for to in self.others(name)
        ]

    def third(self, t):
        name, q = self.axis(t, 1)
        self.arrived(t)
        size = self.size(t, 16)
        total = self.red[t, span(q, size), :]
        for other in self.others(name):
            total = total + self.two[t, other, 0:size, :]
        name, r = self.axis(t, 2)
        self.three[t, r, 0:size, :] = total
        piece = self.three.at[t, r, pl.ds(0, size)]
        self.copies[t] = [self.put(piece, piece, **{name: to}) for to in self.others(name)]

    def rows(self, t, fine):
        p, q = self.axis(t, 0)[1], self.axis(t, 1)[1]
        core = self.at["core"]
        return self.rows_of(t, core, p * 4 + q, self.size(t, 16)) if fine else self.rows_of(t, core, p, self.size(t, 4))

    def spread(self, t, rows, name):
        piece = self.outs[self.matrix(t)].at[rows]
        return [self.put(piece, piece, **{name: to}) for to in self.others(name)]

    def back_second(self, t):
        self.arrived(t)
        size = self.size(t, 16)
        rows = self.rows(t, True)
        total = self.three[t, 0, 0:size, :]
        for slot in range(1, 4):
            total = total + self.three[t, slot, 0:size, :]
        self.outs[self.matrix(t)][rows, :] = total
        self.copies[t] = self.spread(t, rows, self.axis(t, 1)[0])

    def back_first(self, t):
        self.arrived(t)
        rows = self.rows(t, False)
        self.copies[t] = self.spread(t, rows, self.axis(t, 0)[0])
        piece = self.outs[self.matrix(t)].at[rows]
        self.own[t] = self.put(piece, piece, core=1 - self.at["core"])

    def back_cores(self, t):
        p = self.axis(t, 0)[1]
        later = [self.own[t]]
        for d, copy in zip((2, 1, 3), self.copies[t]):
            copy.wait_recv()
            rows = self.rows_of(t, self.at["core"], (p + 4 - d) % 4, self.size(t, 4))
            piece = self.outs[self.matrix(t)].at[rows]
            later.append(self.put(piece, piece, core=1 - self.at["core"]))
        self.copies[t] = later

    def finish(self, t):
        self.arrived(t)

    def drain(self):
        for copy in self.flying:
            copy.wait_send()


class Tally:
    def __init__(self, reducer, ref):
        self.reducer, self.ref, self.copies = reducer, ref, None

    def send(self, k, value):
        axis = ("core", "x", "y", "z")[k]
        at, n = self.reducer.at, 2 if k == 0 else 4
        slot = self.ref.at[k, at[axis]]
        self.ref[k, at[axis]] = value
        self.copies = [self.reducer.put(slot, slot, **{axis: (at[axis] + d) % n}) for d in range(1, n)]

    def total(self, k):
        for copy in self.copies:
            copy.wait_recv()
        total = self.ref[k, 0]
        for slot in range(1, 2 if k == 0 else 4):
            total = total + self.ref[k, slot]
        return total


def step_kernel(
    x_in, w_in_in, w_mid_in, w_out_in, events, tie, entry_in, spread, bit,
    gx_out, go_out, gm_out, gi_out, loss_out,
    sums, x, w_in, w_mid, w_out, x_t, fh_t, hid_t, s1, s2, ind, indp, wb, w, wn, wp, own, prev, hb, hp, nb, pb,
    first_col, firstp_col, entry_col, evt, evp, idxn, logs, g, acc, pair, one, red, two, three, tally,
    in_sem, out_sem, small_send, small_recv, w_send, w_recv, gx_sem, send, recv, *, words, total_rows, chain, streams,
):
    n, wide = x.shape[0], w_out.shape[1]
    parts, part = w.shape[0], w.shape[2]
    tiles, quarters = n // T, n // Q
    at = coordinates()
    me = lax.axis_index("chain")
    strata = lax.axis_index("strata")
    right, left = (strata, (me + 1) % chain), (strata, (me + chain - 1) % chain)

    barrier = pltpu.get_barrier_semaphore()
    friends = [left, right, device(at, core=1 - at["core"])]
    for axis in "xyz":
        friends += [device(at, **{axis: (at[axis] + d) % 4}) for d in range(1, 4)]
    for friend in friends:
        pl.semaphore_signal(barrier, inc=1, device_id=friend, device_id_type=MESH)
    loads = [
        pltpu.make_async_copy(source, target, in_sem.at[k])
        for k, (source, target) in enumerate(((x_in, x), (w_in_in, w_in), (w_mid_in, w_mid), (w_out_in, w_out)))
    ]
    for load in loads:
        load.start()
    evt[0:words, :] = events[...]
    evt[words : words + 1, :] = tie[...] - me * n
    evt[words + 1 : words + 2, :] = entry_in[...] - me * n + n
    evt[words + 2 :, :] = jnp.zeros((evt.shape[0] - words - 2, n), I32)
    pl.semaphore_wait(barrier, len(friends))

    def remote(source, target, s, r, to):
        return pltpu.make_async_remote_copy(
            src_ref=source, dst_ref=target, send_sem=s, recv_sem=r, device_id=to, device_id_type=MESH)

    top = words // 8 * 8
    ev_copy = remote(evt, evp, small_send.at[0], small_recv.at[0], right)
    id_copy = remote(evt.at[pl.ds(top, 8)], idxn, small_send.at[1], small_recv.at[1], left)
    ev_copy.start()
    id_copy.start()

    def to_left(c, r):
        rows = span(r, T)
        return remote(w.at[c, rows], wn.at[c, rows], w_send.at[0, c, r], w_recv.at[0, c, r], left)

    def to_right(c, r):
        rows = span(r, T)
        return remote(w.at[c, rows], wp.at[c, rows], w_send.at[1, c, r], w_recv.at[1, c, r], right)

    logs[...] = jnp.zeros_like(logs)
    for load in loads:
        load.wait()

    def forward(r, _):
        rows = span(r, T)
        pre = dot(x[rows, :], w_in[...])
        s = sigmoid(pre)
        first = (pre * s).astype(BF16)
        s1[rows, :] = (s * (1.0 + pre * (1.0 - s))).astype(BF16)
        mid = dot(first, w_mid[...])
        s = sigmoid(mid)
        hidden = (mid * s).astype(BF16)
        s2[rows, :] = (s * (1.0 + mid * (1.0 - s))).astype(BF16)
        eta = dot(hidden, w_out[...])
        weight = jnp.exp(eta)
        for c in range(parts):
            w[c, rows, :] = weight[:, c * part : (c + 1) * part]
        to_left(0, r).start()
        to_right(0, r).start()
        wb[rows, :] = weight.astype(BF16)
        fh_t[:, rows] = first.T
        hid_t[:, rows] = hidden.T
        value = unpack(evt[:, rows], spread[...])
        flag = jnp.bitwise_and(lax.shift_right_logical(value[:, :wide], bit[...]), 1).astype(F32)
        ind[rows, :] = flag.astype(BF16)
        first_col[rows, :] = value[:, wide : wide + 128]
        entry_col[rows, :] = value[:, wide + 128 : wide + 256]
        logs[...] -= jnp.sum((flag * eta).reshape(-1, 8, wide), axis=0)
        return 0

    lax.fori_loop(0, tiles, forward, 0)

    def later(r, _):
        for c in range(1, parts):
            to_left(c, r).start()
            to_right(c, r).start()
        return 0

    lax.fori_loop(0, tiles, later, 0)

    ev_copy.wait_recv()
    id_copy.wait_recv()
    real = jnp.where(me > 0, 1.0, 0.0).astype(F32)
    idxn[...] = idxn[...] + jnp.where(me == chain - 1, 1 << 20, 0)

    def unpack_prev(r, _):
        rows = span(r, T)
        value = unpack(evp[:, rows], spread[...])
        flag = jnp.bitwise_and(lax.shift_right_logical(value[:, :wide], bit[...]), 1).astype(F32)
        indp[rows, :] = (flag * real).astype(BF16)
        firstp_col[rows, :] = value[:, wide : wide + 128]
        x_t[:, rows] = x[rows, :].T
        return 0

    lax.fori_loop(0, tiles, unpack_prev, 0)

    def lane(base):
        return lax.broadcasted_iota(I32, (Q, 128), 1) + base

    def row(table, k, j, h):
        return table[k : k + 1, j * Q + h * 128 : j * Q + (h + 1) * 128]

    FIRST, ENTRY, ENTRY_N = words, words + 1, words + 1 - top

    def own_part(i, _):
        rows = span(i, Q)
        first, firstp = first_col[rows, :], firstp_col[rows, :]
        total = totalp = 0.0
        for j in range(quarters):
            m = mask(lambda h: (row(evt, ENTRY, j, h) <= first + n) & (first <= lane(j * Q + h * 128)))
            total += dot(m, wb[j * Q : (j + 1) * Q, :])
        for c in range(parts):
            own[c, rows, :] = total[:, c * part : (c + 1) * part]
        for j in range(quarters):
            m = mask(lambda h: row(evt, ENTRY, j, h) <= firstp)
            totalp += dot(m, wb[j * Q : (j + 1) * Q, :])
        for c in range(parts):
            prev[c, rows, :] = totalp[:, c * part : (c + 1) * part]
        return 0

    lax.fori_loop(0, quarters, own_part, 0)

    def add_logs(c):
        cols = slice(c * part, (c + 1) * part)

        def tile(i, _):
            rows = span(i, T)
            log = jnp.where(ind[rows, cols].astype(F32) > 0.0, jnp.log(own[c, rows, :]), 0.0)
            logs[:, cols] += jnp.sum(log.reshape(-1, 8, part), axis=0)
            return 0

        lax.fori_loop(0, tiles, tile, 0)

    eta_ref = wb

    def from_next(c, q):
        for r in range(q * Q // T, (q + 1) * Q // T):
            to_left(c, r).wait_recv()
        nb[...] = wn[c, q * Q : (q + 1) * Q, :].astype(BF16)

        def tile(i, _):
            rows = span(i, Q)
            first = first_col[rows, :]
            own[c, rows, :] += dot(mask(lambda h: row(idxn, ENTRY_N, q, h) <= first), nb[...])
            return 0

        lax.fori_loop(0, quarters, tile, 0)

    def from_previous(c, q):
        for r in range(q * Q // T, (q + 1) * Q // T):
            to_right(c, r).wait_recv()
        pb[...] = wp[c, q * Q : (q + 1) * Q, :].astype(BF16)

        def tile(i, _):
            rows = span(i, Q)
            firstp = firstp_col[rows, :]
            m = mask(lambda h: (row(evp, ENTRY, q, h) <= firstp + n) & (firstp <= lane(q * Q + h * 128)))
            prev[c, rows, :] += dot(m, pb[...])
            return 0

        lax.fori_loop(0, quarters, tile, 0)

    def hazards(flags, divisors, target):
        def tile(i, _):
            rows = span(i, T)
            flag = flags(rows).astype(F32) > 0.0
            target[rows, :] = jnp.where(flag, 1.0 / divisors(rows), 0.0).astype(BF16)
            return 0

        lax.fori_loop(0, tiles, tile, 0, unroll=2)

    for c in range(parts):
        cols = slice(c * part, (c + 1) * part)
        for q in range(quarters):
            from_next(c, q)
            if q < quarters - 1:
                from_previous(c, q)
        hazards(lambda rows: ind[rows, cols], lambda rows: own[c, rows, :], hb)

        def expose_own(j, _):
            rows = span(j, Q)
            entry = entry_col[rows, :]
            here = lax.broadcasted_iota(I32, (Q, 128), 0) + j * Q
            total = 0.0
            for i in range(quarters):
                m = mask(lambda h: (entry <= row(evt, FIRST, i, h) + n) & (row(evt, FIRST, i, h) <= here))
                total += dot(m, hb[i * Q : (i + 1) * Q, :])
            wn[c, rows, :] = total
            return 0

        lax.fori_loop(0, quarters, expose_own, 0)
        from_previous(c, quarters - 1)
        hazards(lambda rows: indp[rows, cols], lambda rows: prev[c, rows, :], hp)

        def expose(j, _):
            rows = span(j, Q)
            entry = entry_col[rows, :]
            total = wn[c, rows, :]
            for i in range(quarters):
                total += dot(mask(lambda h: entry <= row(evp, FIRST, i, h)), hp[i * Q : (i + 1) * Q, :])
            eta_ref[rows, cols] = (w[c, rows, :] * total - ind[rows, cols].astype(F32)).astype(BF16)
            return 0

        lax.fori_loop(0, quarters, expose, 0, unroll=True)
        g[0, :, cols] = dot(hid_t[...], eta_ref[:, cols])
        if c < parts - 1:
            add_logs(c)

    mid_ref, pre_ref, gx = s2, s1, x
    reducer = Reducer(at, total_rows ** (-0.5), streams, [g.at[t] for t in range(3)], [sums.at[t] for t in range(3)],
                      acc, pair, one, red, two, three, send, recv)
    counted = Tally(reducer, tally)

    outs = [pltpu.make_async_copy(sums.at[t], out, out_sem.at[t]) for t, out in enumerate((go_out, gm_out, gi_out))]

    def advance(t, k):
        if 0 <= k < len(reducer.stages):
            for v, stream in enumerate(streams):
                if stream[0] == t:
                    reducer.stages[k](v)
            if k == len(reducer.stages) - 1:
                outs[t].start()

    def turn(k):
        for t in range(2, -1, -1):
            advance(t, k - t)

    advance(0, 0)

    def middle(i, _):
        rows = span(i, Q)
        mid_grad = dot(eta_ref[rows, :], w_out[...], ((1,), (1,))) * s2[rows, :].astype(F32)
        mid_ref[rows, :] = mid_grad.astype(BF16)
        return 0

    lax.fori_loop(0, quarters, middle, 0, unroll=True)
    advance(0, 1)
    half = g.shape[1] // 2
    away, kept = span(1 - at["core"], half), span(at["core"], half)
    g[1, away, :] = dot(fh_t[away, :], mid_ref[...])
    advance(1, 0)
    g[1, kept, :] = dot(fh_t[kept, :], mid_ref[...])

    def inner(i, _):
        rows = span(i, Q)
        pre_grad = dot(mid_ref[rows, :], w_mid[...], ((1,), (1,))) * s1[rows, :].astype(F32)
        pre_ref[rows, :] = pre_grad.astype(BF16)
        return 0

    lax.fori_loop(0, quarters, inner, 0, unroll=True)
    advance(1, 1)
    g[2, away, :] = dot(x_t[away, :], pre_ref[...])
    advance(2, 0)
    g[2, kept, :] = dot(x_t[kept, :], pre_ref[...])
    advance(0, 2)

    def last(i, _):
        rows = span(i, Q)
        gx[rows, :] = dot(pre_ref[rows, :], w_in[...], ((1,), (1,))).astype(BF16)
        return 0

    advance(2, 1)
    add_logs(parts - 1)
    counted.send(0, logs[...] / total_rows)
    advance(1, 2)
    advance(0, 3)
    lax.fori_loop(0, quarters, last, 0)
    gx_copy = pltpu.make_async_copy(gx, gx_out, gx_sem)
    gx_copy.start()
    for k in range(4, 7):
        turn(k)
        counted.send(k - 3, counted.total(k - 4))
    turn(7)
    loss_out[...] = jnp.sum(counted.total(3), axis=0, keepdims=True)
    for k in range(8, len(reducer.stages) + 2):
        turn(k)
    reducer.drain()
    gx_copy.wait()
    for out in outs:
        out.wait()
    ev_copy.wait_send()
    id_copy.wait_send()

    def drain(r, _):
        for c in range(parts):
            to_left(c, r).wait_send()
            to_right(c, r).wait_send()
        return 0

    lax.fori_loop(0, tiles, drain, 0)


def copy_kernel(*refs):
    m = (len(refs) - 2) // 3
    sources, targets, buffers, sem_in, sem_out = refs[:m], refs[m : 2 * m], refs[2 * m : 3 * m], refs[-2], refs[-1]
    reads, writes = [], []
    for source, target, buffer in zip(sources, targets, buffers):
        pieces = max(source.shape[0] // 256, 1) if source.dtype == F32 else source.shape[0] // 512
        size = source.shape[0] // pieces
        for k in range(pieces):
            at = pl.ds(k * size, size)
            i = len(reads)
            reads.append(pltpu.make_async_copy(source.at[at], buffer.at[at], sem_in.at[i]))
            writes.append(pltpu.make_async_copy(buffer.at[at], target.at[at], sem_out.at[i]))
    for read in reads:
        read.start()
    for read, write in zip(reads, writes):
        read.wait()
        write.start()
    for write in writes:
        write.wait()


def on_device(features, events, tie_first, entry_row, w_in, w_mid, w_out):
    n, width = features.shape
    hidden_width, wide = w_out.shape
    words = events.shape[1]
    chain, strata = lax.axis_size("chain"), lax.axis_size("strata")
    assert (width, hidden_width, wide, n % Q) == (512, 512, 512, 0) and words % 8 in range(1, 7)
    parts = 2
    part = wide // parts
    deep = words // 8 * 8 + 8
    column = np.arange(wide + 256)
    source = np.where(column < wide, column // WORD_BITS, words + (column - wide) // 128)
    spread = jnp.asarray((source[None, :] == np.arange(deep)[:, None]).astype(np.float32), BF16)
    bit = jnp.asarray((np.arange(wide) % WORD_BITS)[None, :].astype(np.int32))

    m = 3
    half = hidden_width // 2
    large = half // 2
    streams = tuple((t, v * large, large, (2 * t + v) % 3) for t in range(m) for v in range(2))
    many = len(streams)
    messages = many * 20 + 10
    V = pltpu.VMEM
    dma = pltpu.SemaphoreType.DMA
    by_rows, by_columns, square = V((n, wide), BF16), V((wide, n), BF16), V((wide, wide), BF16)
    scratch = (
        [V((m, hidden_width, wide), F32), by_rows] + [square] * 3 + [by_columns] * 3 + [by_rows] * 5
        + [V((parts, n, part), F32)] * 5
        + [V((n, part), BF16)] * 2 + [V((Q, part), BF16)] * 2 + [V((n, 128), I32)] * 3
        + [V((deep, n), I32)] * 2 + [V((8, n), I32), V((8, wide), F32), V((m, hidden_width, wide), F32)]
        + [V((many, large, wide), F32)] * 2
        + [V((many, 4, large // 4, wide), F32), V((many, large // 4, wide), F32)]
        + [V((many, 4, large // 16, wide), F32)] * 2 + [V((4, 4, 8, wide), F32)]
        + [dma((4,)), dma((m,))] + [dma((2,))] * 2 + [dma((2, parts, n // T))] * 2 + [dma, dma((messages,)), dma((messages,))]
    )
    vmem = pl.BlockSpec(memory_space=V)
    anywhere = pl.BlockSpec(memory_space=pl.ANY)
    grad = jax.ShapeDtypeStruct((hidden_width, wide), F32)
    shapes = [jax.ShapeDtypeStruct((n, width), BF16), grad, grad, grad, jax.ShapeDtypeStruct((1, wide), F32)]
    results = pl.pallas_call(
        functools.partial(step_kernel, words=words, total_rows=n * chain * strata, chain=chain, streams=streams),
        in_specs=[anywhere] * 4 + [vmem] * 5,
        out_specs=[anywhere] * 4 + [vmem],
        out_shape=shapes,
        scratch_shapes=scratch,
        compiler_params=pltpu.CompilerParams(
            collective_id=0, has_side_effects=True, vmem_limit_bytes=67043328),
        name="step",
    )(features, w_in, w_mid, w_out, events.T, tie_first[None], entry_row[None], spread, bit)
    gx, go, gm, gi, loss = pl.pallas_call(
        copy_kernel,
        in_specs=[anywhere] * 5,
        out_specs=[anywhere] * 5,
        out_shape=shapes,
        scratch_shapes=[V(shape.shape, shape.dtype) for shape in shapes] + [dma((16,))] * 2,
        name="results",
    )(*results)
    return (loss[0], gx, gi, gm, go)


def solution(mesh):
    placed = (
        P(("strata", "chain"), None),
        P(("strata", "chain"), None),
        P(("strata", "chain")),
        P(("strata", "chain")),
        P(),
        P(),
        P(),
    )
    return jax.shard_map(
        on_device,
        mesh=mesh,
        in_specs=placed,
        out_specs=(P(), P(("strata", "chain"), None), P(), P(), P()),
        check_vma=False,
    )
```

```python
import functools

import jax
import jax.numpy as jnp
import numpy as np
from jax import lax
from jax.experimental import pallas as pl
from jax.experimental.pallas import tpu as pltpu
from jax.sharding import PartitionSpec as P

T = 256
Q = 512
WORD_BITS = 15
F32 = jnp.float32
BF16 = jnp.bfloat16
I32 = jnp.int32
MESH = pl.DeviceIdType.MESH


def sigmoid(v):
    return 0.5 * jnp.tanh(0.5 * v) + 0.5


def span(i, size):
    return pl.ds(pl.multiple_of(i * size, size), size)


def dot(a, b, contract=((1,), (0,))):
    return lax.dot_general(a, b, (contract, ((), ())), preferred_element_type=F32)


def mask(build):
    return jnp.concatenate([jnp.where(build(h), 1.0, 0.0).astype(BF16) for h in range(Q // 128)], axis=1)


def unpack(words, table):
    hi = lax.shift_right_logical(words, 8).astype(F32).astype(BF16)
    lo = jnp.bitwise_and(words, 255).astype(F32).astype(BF16)
    value = dot(hi, table, ((0,), (0,))) * 256.0 + dot(lo, table, ((0,), (0,)))
    return value.astype(I32)


def coordinates():
    s, c = lax.axis_index("strata"), lax.axis_index("chain")
    return {"y": s // 2, "core": s % 2, "z": c // 4, "x": c % 4}


def device(at, **moved):
    at = {**at, **moved}
    return (at["y"] * 2 + at["core"], at["z"] * 4 + at["x"])


class Reducer:
    def __init__(self, at, factor, streams, given, outs, acc, pair, one, red, two, three, send, recv):
        self.at, self.factor, self.streams, self.given, self.outs = at, factor, streams, given, outs
        self.acc, self.pair, self.one, self.red, self.two, self.three = acc, pair, one, red, two, three
        self.send, self.recv = send, recv
        self.count, self.flying, self.copies, self.own = 0, [], {}, {}
        self.half = given[0].shape[0] // 2
        self.stages = [self.cores, self.first, self.second, self.third, self.back_second, self.back_first,
                       self.back_cores, self.finish]

    def put(self, source, target, **moved):
        k, self.count = self.count, self.count + 1
        copy = pltpu.make_async_remote_copy(
            src_ref=source, dst_ref=target, send_sem=self.send.at[k], recv_sem=self.recv.at[k],
            device_id=device(self.at, **moved), device_id_type=MESH,
        )
        copy.start()
        self.flying.append(copy)
        return copy

    def matrix(self, t):
        return self.streams[t][0]

    def size(self, t, cut=1):
        return self.streams[t][2] // cut

    def axis(self, t, k):
        name = "xyz"[(self.streams[t][3] + k) % 3]
        return name, self.at[name]

    def others(self, name):
        return [(self.at[name] + d) % 4 for d in (2, 1, 3)]

    def rows_of(self, t, core, start, size):
        return span(core * (self.half // size) + self.streams[t][1] // size + start, size)

    def arrived(self, t):
        for copy in self.copies[t]:
            copy.wait_recv()

    def cores(self, t):
        core, size = self.at["core"], self.size(t)
        away = self.rows_of(t, 1 - core, 0, size)
        self.copies[t] = [
            self.put(self.given[self.matrix(t)].at[away], self.pair.at[t, pl.ds(0, size)], core=1 - core)
        ]

    def first(self, t):
        name, p = self.axis(t, 0)
        self.arrived(t)
        size = self.size(t)
        kept = self.rows_of(t, self.at["core"], 0, size)
        self.acc[t, 0:size, :] = (self.given[self.matrix(t)][kept, :] + self.pair[t, 0:size, :]) * self.factor
        size = self.size(t, 4)
        self.copies[t] = [
            self.put(self.acc.at[t, span(to, size)], self.one.at[t, p, pl.ds(0, size)], **{name: to})
            for to in self.others(name)
        ]

    def second(self, t):
        name, p = self.axis(t, 0)
        self.arrived(t)
        size = self.size(t, 4)
        total = self.acc[t, span(p, size), :]
        for other in self.others(name):
            total = total + self.one[t, other, 0:size, :]
        self.red[t, 0:size, :] = total
        name, q = self.axis(t, 1)
        size = self.size(t, 16)
        self.copies[t] = [
            self.put(self.red.at[t, span(to, size)], self.two.at[t, q, pl.ds(0, size)], **{name: to})
            for to in self.others(name)
        ]

    def third(self, t):
        name, q = self.axis(t, 1)
        self.arrived(t)
        size = self.size(t, 16)
        total = self.red[t, span(q, size), :]
        for other in self.others(name):
            total = total + self.two[t, other, 0:size, :]
        name, r = self.axis(t, 2)
        self.three[t, r, 0:size, :] = total
        piece = self.three.at[t, r, pl.ds(0, size)]
        self.copies[t] = [self.put(piece, piece, **{name: to}) for to in self.others(name)]

    def rows(self, t, fine):
        p, q = self.axis(t, 0)[1], self.axis(t, 1)[1]
        core = self.at["core"]
        return self.rows_of(t, core, p * 4 + q, self.size(t, 16)) if fine else self.rows_of(t, core, p, self.size(t, 4))

    def spread(self, t, rows, name):
        piece = self.outs[self.matrix(t)].at[rows]
        return [self.put(piece, piece, **{name: to}) for to in self.others(name)]

    def back_second(self, t):
        self.arrived(t)
        size = self.size(t, 16)
        rows = self.rows(t, True)
        total = self.three[t, 0, 0:size, :]
        for slot in range(1, 4):
            total = total + self.three[t, slot, 0:size, :]
        self.outs[self.matrix(t)][rows, :] = total
        self.copies[t] = self.spread(t, rows, self.axis(t, 1)[0])

    def back_first(self, t):
        self.arrived(t)
        rows = self.rows(t, False)
        self.copies[t] = self.spread(t, rows, self.axis(t, 0)[0])
        piece = self.outs[self.matrix(t)].at[rows]
        self.own[t] = self.put(piece, piece, core=1 - self.at["core"])

    def back_cores(self, t):
        p = self.axis(t, 0)[1]
        later = [self.own[t]]
        for d, copy in zip((2, 1, 3), self.copies[t]):
            copy.wait_recv()
            rows = self.rows_of(t, self.at["core"], (p + 4 - d) % 4, self.size(t, 4))
            piece = self.outs[self.matrix(t)].at[rows]
            later.append(self.put(piece, piece, core=1 - self.at["core"]))
        self.copies[t] = later

    def finish(self, t):
        self.arrived(t)

    def drain(self):
        for copy in self.flying:
            copy.wait_send()


class Tally:
    def __init__(self, reducer, ref):
        self.reducer, self.ref, self.copies = reducer, ref, None

    def send(self, k, value):
        axis = ("core", "x", "y", "z")[k]
        at, n = self.reducer.at, 2 if k == 0 else 4
        slot = self.ref.at[k, at[axis]]
        self.ref[k, at[axis]] = value
        self.copies = [self.reducer.put(slot, slot, **{axis: (at[axis] + d) % n}) for d in range(1, n)]

    def total(self, k):
        for copy in self.copies:
            copy.wait_recv()
        total = self.ref[k, 0]
        for slot in range(1, 2 if k == 0 else 4):
            total = total + self.ref[k, slot]
        return total


def step_kernel(
    x_in, w_in_in, w_mid_in, w_out_in, events_in, tie_in, entry_in, spread_in, bit_in,
    gx_out, go_out, gm_out, gi_out, loss_out,
    events, tie, entry_rows, spread, bit, sums, x, w_in, w_mid, w_out, x_t, fh_t, hid_t, s1, s2, ind, indp, wb, w, wn, wp, own, prev, hb, hp, nb, pb,
    first_col, firstp_col, entry_col, evt, evp, idxn, logs, g, acc, pair, one, red, two, three, tally,
    in_sem, out_sem, small_send, small_recv, w_send, w_recv, gx_sem, send, recv, *, words, total_rows, chain, streams,
):
    n, wide = x.shape[0], w_out.shape[1]
    parts, part = w.shape[0], w.shape[2]
    tiles, quarters = n // T, n // Q
    at = coordinates()
    me = lax.axis_index("chain")
    strata = lax.axis_index("strata")
    right, left = (strata, (me + 1) % chain), (strata, (me + chain - 1) % chain)

    barrier = pltpu.get_barrier_semaphore()
    friends = [left, right, device(at, core=1 - at["core"])]
    for axis in "xyz":
        friends += [device(at, **{axis: (at[axis] + d) % 4}) for d in range(1, 4)]
    for friend in friends:
        pl.semaphore_signal(barrier, inc=1, device_id=friend, device_id_type=MESH)
    loads = [
        pltpu.make_async_copy(source, target, in_sem.at[k])
        for k, (source, target) in enumerate((
            (events_in, events), (tie_in, tie), (entry_in, entry_rows), (w_in_in, w_in), (x_in, x),
            (w_mid_in, w_mid), (w_out_in, w_out), (spread_in, spread), (bit_in, bit)))
    ]
    for load in loads:
        load.start()
    for load in loads[:3]:
        load.wait()
    evt[0:words, :] = events[...]
    evt[words : words + 1, :] = tie[...] - me * n
    evt[words + 1 : words + 2, :] = entry_rows[...] - me * n + n
    evt[words + 2 :, :] = jnp.zeros((evt.shape[0] - words - 2, n), I32)
    pl.semaphore_wait(barrier, len(friends))

    def remote(source, target, s, r, to):
        return pltpu.make_async_remote_copy(
            src_ref=source, dst_ref=target, send_sem=s, recv_sem=r, device_id=to, device_id_type=MESH)

    top = words // 8 * 8
    ev_copy = remote(evt, evp, small_send.at[0], small_recv.at[0], right)
    id_copy = remote(evt.at[pl.ds(top, 8)], idxn, small_send.at[1], small_recv.at[1], left)
    ev_copy.start()
    id_copy.start()

    def to_left(c, r):
        rows = span(r, T)
        return remote(w.at[c, rows], wn.at[c, rows], w_send.at[0, c, r], w_recv.at[0, c, r], left)

    def to_right(c, r):
        rows = span(r, T)
        return remote(w.at[c, rows], wp.at[c, rows], w_send.at[1, c, r], w_recv.at[1, c, r], right)

    logs[...] = jnp.zeros_like(logs)
    for load in loads[3:]:
        load.wait()

    def forward(r, _):
        rows = span(r, T)
        pre = dot(x[rows, :], w_in[...])
        s = sigmoid(pre)
        first = (pre * s).astype(BF16)
        s1[rows, :] = (s * (1.0 + pre * (1.0 - s))).astype(BF16)
        mid = dot(first, w_mid[...])
        s = sigmoid(mid)
        hidden = (mid * s).astype(BF16)
        s2[rows, :] = (s * (1.0 + mid * (1.0 - s))).astype(BF16)
        eta = dot(hidden, w_out[...])
        weight = jnp.exp(eta)
        for c in range(parts):
            w[c, rows, :] = weight[:, c * part : (c + 1) * part]
        to_left(0, r).start()
        to_right(0, r).start()
        wb[rows, :] = weight.astype(BF16)
        fh_t[:, rows] = first.T
        hid_t[:, rows] = hidden.T
        value = unpack(evt[:, rows], spread[...])
        flag = jnp.bitwise_and(lax.shift_right_logical(value[:, :wide], bit[...]), 1).astype(F32)
        ind[rows, :] = flag.astype(BF16)
        first_col[rows, :] = value[:, wide : wide + 128]
        entry_col[rows, :] = value[:, wide + 128 : wide + 256]
        logs[...] -= jnp.sum((flag * eta).reshape(-1, 8, wide), axis=0)
        return 0

    lax.fori_loop(0, tiles, forward, 0)

    def later(r, _):
        for c in range(1, parts):
            to_left(c, r).start()
            to_right(c, r).start()
        return 0

    lax.fori_loop(0, tiles, later, 0)

    ev_copy.wait_recv()
    id_copy.wait_recv()
    real = jnp.where(me > 0, 1.0, 0.0).astype(F32)
    idxn[...] = idxn[...] + jnp.where(me == chain - 1, 1 << 20, 0)

    def unpack_prev(r, _):
        rows = span(r, T)
        value = unpack(evp[:, rows], spread[...])
        flag = jnp.bitwise_and(lax.shift_right_logical(value[:, :wide], bit[...]), 1).astype(F32)
        indp[rows, :] = (flag * real).astype(BF16)
        firstp_col[rows, :] = value[:, wide : wide + 128]
        x_t[:, rows] = x[rows, :].T
        return 0

    lax.fori_loop(0, tiles, unpack_prev, 0)

    def lane(base):
        return lax.broadcasted_iota(I32, (Q, 128), 1) + base

    def row(table, k, j, h):
        return table[k : k + 1, j * Q + h * 128 : j * Q + (h + 1) * 128]

    FIRST, ENTRY, ENTRY_N = words, words + 1, words + 1 - top

    def own_part(i, _):
        rows = span(i, Q)
        first, firstp = first_col[rows, :], firstp_col[rows, :]
        total = totalp = 0.0
        for j in range(quarters):
            m = mask(lambda h: (row(evt, ENTRY, j, h) <= first + n) & (first <= lane(j * Q + h * 128)))
            total += dot(m, wb[j * Q : (j + 1) * Q, :])
        for c in range(parts):
            own[c, rows, :] = total[:, c * part : (c + 1) * part]
        for j in range(quarters):
            m = mask(lambda h: row(evt, ENTRY, j, h) <= firstp)
            totalp += dot(m, wb[j * Q : (j + 1) * Q, :])
        for c in range(parts):
            prev[c, rows, :] = totalp[:, c * part : (c + 1) * part]
        return 0

    lax.fori_loop(0, quarters, own_part, 0)

    def add_logs(c):
        cols = slice(c * part, (c + 1) * part)

        def tile(i, _):
            rows = span(i, T)
            log = jnp.where(ind[rows, cols].astype(F32) > 0.0, jnp.log(own[c, rows, :]), 0.0)
            logs[:, cols] += jnp.sum(log.reshape(-1, 8, part), axis=0)
            return 0

        lax.fori_loop(0, tiles, tile, 0)

    eta_ref = wb

    def from_next(c, q):
        for r in range(q * Q // T, (q + 1) * Q // T):
            to_left(c, r).wait_recv()
        nb[...] = wn[c, q * Q : (q + 1) * Q, :].astype(BF16)

        def tile(i, _):
            rows = span(i, Q)
            first = first_col[rows, :]
            own[c, rows, :] += dot(mask(lambda h: row(idxn, ENTRY_N, q, h) <= first), nb[...])
            return 0

        lax.fori_loop(0, quarters, tile, 0)

    def from_previous(c, q):
        for r in range(q * Q // T, (q + 1) * Q // T):
            to_right(c, r).wait_recv()
        pb[...] = wp[c, q * Q : (q + 1) * Q, :].astype(BF16)

        def tile(i, _):
            rows = span(i, Q)
            firstp = firstp_col[rows, :]
            m = mask(lambda h: (row(evp, ENTRY, q, h) <= firstp + n) & (firstp <= lane(q * Q + h * 128)))
            prev[c, rows, :] += dot(m, pb[...])
            return 0

        lax.fori_loop(0, quarters, tile, 0)

    def hazards(flags, divisors, target):
        def tile(i, _):
            rows = span(i, T)
            flag = flags(rows).astype(F32) > 0.0
            target[rows, :] = jnp.where(flag, 1.0 / divisors(rows), 0.0).astype(BF16)
            return 0

        lax.fori_loop(0, tiles, tile, 0, unroll=2)

    for c in range(parts):
        cols = slice(c * part, (c + 1) * part)
        for q in range(quarters):
            from_next(c, q)
            if q < quarters - 1:
                from_previous(c, q)
        hazards(lambda rows: ind[rows, cols], lambda rows: own[c, rows, :], hb)

        def expose_own(j, _):
            rows = span(j, Q)
            entry = entry_col[rows, :]
            here = lax.broadcasted_iota(I32, (Q, 128), 0) + j * Q
            total = 0.0
            for i in range(quarters):
                m = mask(lambda h: (entry <= row(evt, FIRST, i, h) + n) & (row(evt, FIRST, i, h) <= here))
                total += dot(m, hb[i * Q : (i + 1) * Q, :])
            wn[c, rows, :] = total
            return 0

        lax.fori_loop(0, quarters, expose_own, 0)
        from_previous(c, quarters - 1)
        hazards(lambda rows: indp[rows, cols], lambda rows: prev[c, rows, :], hp)

        def expose(j, _):
            rows = span(j, Q)
            entry = entry_col[rows, :]
            total = wn[c, rows, :]
            for i in range(quarters):
                total += dot(mask(lambda h: entry <= row(evp, FIRST, i, h)), hp[i * Q : (i + 1) * Q, :])
            eta_ref[rows, cols] = (w[c, rows, :] * total - ind[rows, cols].astype(F32)).astype(BF16)
            return 0

        lax.fori_loop(0, quarters, expose, 0, unroll=True)
        g[0, :, cols] = dot(hid_t[...], eta_ref[:, cols])
        if c < parts - 1:
            add_logs(c)

    mid_ref, pre_ref, gx = s2, s1, x
    reducer = Reducer(at, total_rows ** (-0.5), streams, [g.at[t] for t in range(3)], [sums.at[t] for t in range(3)],
                      acc, pair, one, red, two, three, send, recv)
    counted = Tally(reducer, tally)

    outs = [pltpu.make_async_copy(sums.at[t], out, out_sem.at[t]) for t, out in enumerate((go_out, gm_out, gi_out))]

    def advance(t, k):
        if 0 <= k < len(reducer.stages):
            for v, stream in enumerate(streams):
                if stream[0] == t:
                    reducer.stages[k](v)
            if k == len(reducer.stages) - 1:
                outs[t].start()

    def turn(k):
        for t in range(2, -1, -1):
            advance(t, k - t)

    advance(0, 0)

    def middle(i, _):
        rows = span(i, Q)
        mid_grad = dot(eta_ref[rows, :], w_out[...], ((1,), (1,))) * s2[rows, :].astype(F32)
        mid_ref[rows, :] = mid_grad.astype(BF16)
        return 0

    lax.fori_loop(0, quarters, middle, 0, unroll=True)
    advance(0, 1)
    half = g.shape[1] // 2
    away, kept = span(1 - at["core"], half), span(at["core"], half)
    g[1, away, :] = dot(fh_t[away, :], mid_ref[...])
    advance(1, 0)
    g[1, kept, :] = dot(fh_t[kept, :], mid_ref[...])

    def inner(i, _):
        rows = span(i, Q)
        pre_grad = dot(mid_ref[rows, :], w_mid[...], ((1,), (1,))) * s1[rows, :].astype(F32)
        pre_ref[rows, :] = pre_grad.astype(BF16)
        return 0

    lax.fori_loop(0, quarters, inner, 0, unroll=True)
    advance(1, 1)
    g[2, away, :] = dot(x_t[away, :], pre_ref[...])
    advance(2, 0)
    g[2, kept, :] = dot(x_t[kept, :], pre_ref[...])
    advance(0, 2)

    def last(i, _):
        rows = span(i, Q)
        gx[rows, :] = dot(pre_ref[rows, :], w_in[...], ((1,), (1,))).astype(BF16)
        return 0

    advance(2, 1)
    add_logs(parts - 1)
    counted.send(0, logs[...] / total_rows)
    advance(1, 2)
    advance(0, 3)
    lax.fori_loop(0, quarters, last, 0)
    gx_copy = pltpu.make_async_copy(gx, gx_out, gx_sem)
    gx_copy.start()
    for k in range(4, 7):
        turn(k)
        counted.send(k - 3, counted.total(k - 4))
    turn(7)
    loss_out[...] = jnp.sum(counted.total(3), axis=0, keepdims=True)
    for k in range(8, len(reducer.stages) + 2):
        turn(k)
    reducer.drain()
    gx_copy.wait()
    for out in outs:
        out.wait()
    ev_copy.wait_send()
    id_copy.wait_send()

    def drain(r, _):
        for c in range(parts):
            to_left(c, r).wait_send()
            to_right(c, r).wait_send()
        return 0

    lax.fori_loop(0, tiles, drain, 0)


def copy_kernel(*refs):
    m = (len(refs) - 2) // 3
    sources, targets, buffers, sem_in, sem_out = refs[:m], refs[m : 2 * m], refs[2 * m : 3 * m], refs[-2], refs[-1]
    reads, writes = [], []
    for source, target, buffer in zip(sources, targets, buffers):
        pieces = max(source.shape[0] // 128, 1) if source.dtype == F32 else source.shape[0] // 256
        size = source.shape[0] // pieces
        for k in range(pieces):
            at = pl.ds(k * size, size)
            i = len(reads)
            reads.append(pltpu.make_async_copy(source.at[at], buffer.at[at], sem_in.at[i]))
            writes.append(pltpu.make_async_copy(buffer.at[at], target.at[at], sem_out.at[i]))
    for read in reads:
        read.start()
    for read, write in zip(reads, writes):
        read.wait()
        write.start()
    for write in writes:
        write.wait()


def on_device(features, events, tie_first, entry_row, w_in, w_mid, w_out):
    n, width = features.shape
    hidden_width, wide = w_out.shape
    words = events.shape[1]
    chain, strata = lax.axis_size("chain"), lax.axis_size("strata")
    assert (width, hidden_width, wide, n % Q) == (512, 512, 512, 0) and words % 8 in range(1, 7)
    parts = 2
    part = wide // parts
    deep = words // 8 * 8 + 8
    column = np.arange(wide + 256)
    source = np.where(column < wide, column // WORD_BITS, words + (column - wide) // 128)
    spread = jnp.asarray((source[None, :] == np.arange(deep)[:, None]).astype(np.float32), BF16)
    bit = jnp.asarray((np.arange(wide) % WORD_BITS)[None, :].astype(np.int32))

    m = 3
    half = hidden_width // 2
    large = half // 2
    streams = tuple((t, v * large, large, (2 * t + v) % 3) for t in range(m) for v in range(2))
    many = len(streams)
    messages = many * 20 + 10
    V = pltpu.VMEM
    dma = pltpu.SemaphoreType.DMA
    by_rows, by_columns, square = V((n, wide), BF16), V((wide, n), BF16), V((wide, wide), BF16)
    scratch = (
        [V((words, n), I32), V((1, n), I32), V((1, n), I32), V(spread.shape, BF16), V(bit.shape, I32)]
        + [V((m, hidden_width, wide), F32), by_rows] + [square] * 3 + [by_columns] * 3 + [by_rows] * 5
        + [V((parts, n, part), F32)] * 5
        + [V((n, part), BF16)] * 2 + [V((Q, part), BF16)] * 2 + [V((n, 128), I32)] * 3
        + [V((deep, n), I32)] * 2 + [V((8, n), I32), V((8, wide), F32), V((m, hidden_width, wide), F32)]
        + [V((many, large, wide), F32)] * 2
        + [V((many, 4, large // 4, wide), F32), V((many, large // 4, wide), F32)]
        + [V((many, 4, large // 16, wide), F32)] * 2 + [V((4, 4, 8, wide), F32)]
        + [dma((9,)), dma((m,))] + [dma((2,))] * 2 + [dma((2, parts, n // T))] * 2 + [dma, dma((messages,)), dma((messages,))]
    )
    vmem = pl.BlockSpec(memory_space=V)
    anywhere = pl.BlockSpec(memory_space=pl.ANY)
    grad = jax.ShapeDtypeStruct((hidden_width, wide), F32)
    shapes = [jax.ShapeDtypeStruct((n, width), BF16), grad, grad, grad, jax.ShapeDtypeStruct((1, wide), F32)]
    results = pl.pallas_call(
        functools.partial(step_kernel, words=words, total_rows=n * chain * strata, chain=chain, streams=streams),
        in_specs=[anywhere] * 9,
        out_specs=[anywhere] * 4 + [vmem],
        out_shape=shapes,
        scratch_shapes=scratch,
        compiler_params=pltpu.CompilerParams(
            collective_id=0, has_side_effects=True, vmem_limit_bytes=67043328),
        name="step",
    )(features, w_in, w_mid, w_out, events.T, tie_first[None], entry_row[None], spread, bit)
    gx, go, gm, gi, loss = pl.pallas_call(
        copy_kernel,
        in_specs=[anywhere] * 5,
        out_specs=[anywhere] * 5,
        out_shape=shapes,
        scratch_shapes=[V(shape.shape, shape.dtype) for shape in shapes] + [dma((24,))] * 2,
        name="results",
    )(*results)
    return (loss[0], gx, gi, gm, go)


def solution(mesh):
    placed = (
        P(("strata", "chain"), None),
        P(("strata", "chain"), None),
        P(("strata", "chain")),
        P(("strata", "chain")),
        P(),
        P(),
        P(),
    )
    return jax.shard_map(
        on_device,
        mesh=mesh,
        in_specs=placed,
        out_specs=(P(), P(("strata", "chain"), None), P(), P(), P()),
        check_vma=False,
    )
```
